256 devices in a mesh: tile: 32 (over z_hi, x, core), lev: 4 (over y), sec: 2 (over z_lo).
Axes of the slice: x: 4, y: 4, z: 8 (z_hi: 4, z_lo: 2; z = z_hi * 2 + z_lo), core: 2. Of those that a mesh axis runs over, the one named last changes fastest.
Arguments:
- forcing: float32 [8, 72, 1280, 384], P('sec', 'lev', 'tile'), may hold values from -6 to 6
- courant_x: bfloat16 [72, 1280, 384], P('lev', 'tile'), may hold values from -0.44921875 to 0.44921875
- courant_y: bfloat16 [72, 1280, 384], P('lev', 'tile'), may hold values from -0.44921875 to 0.44921875
- mass_flux: bfloat16 [72, 1280, 384], P('lev', 'tile'), may hold values from 0 to 0.59765625
- limiter_code: int32 [72, 1280, 384], P('lev', 'tile'), may hold values from 0 to 15
- seam_code: int32 [32, 2], replicated, may hold values from 0 to 1
- level_weight: float32 [72], P('lev'), may hold values from 0.02 to 0.5
- sector_share: float32 [8, 1280, 384], P('sec', 'tile'), may hold values from 0.1 to 1
- flux_cell: int32 [1024, 480], P('tile'), may hold values from 0 to 15359
Outputs:
- adjoint_start: float32 [8, 72, 1280, 384], P('sec', 'lev', 'tile')
- flux_sensitivity: float32 [491520], P('tile')
The draws below stay inside these ranges and needn't reach their ends.
All inputs are finite; a program needn't handle non-finite values.
Results may differ from the reference program's by a relative error of at most 0.0003.
Values sent between devices are 32-bit elements; how exact they have to be, the bound alone decides.
A program may use at most 128 MiB of HBM per device.

```python
import math
import jax
import jax.numpy as jnp
from jax import lax

SECTORS = 8
LEVELS = 72
CX = 40
CY = 384
TILES = 32
NX = 1280
SHARE = 480
FL_DEV = 15360
FLUX = 491520


def set_ends(result, rng, smallest, largest):
    place = [jax.random.randint(jax.random.fold_in(rng, axis), (), 0, length) for axis, length in enumerate(result.shape)]
    widest = result.shape.index(max(result.shape))
    beside = place[:widest] + [(place[widest] + 1) % result.shape[widest]] + place[widest + 1:]
    return result.at[tuple(place)].set(smallest).at[tuple(beside)].set(largest)


def levels(rng, extent, cuts, least, high):
    factor_of = 1.0
    for position, blocks in cuts:
        heights = jax.random.uniform(jax.random.fold_in(jax.random.fold_in(rng, 6), position), (blocks,), jnp.float32, least / len(cuts), high / len(cuts))
        factor_of = factor_of * jnp.repeat(jnp.exp(heights), extent[position] // blocks).reshape((-1,) + (1,) * (len(extent) - 1 - position))
    return factor_of


def noise(key, extent, scale, limit, cuts=(), kind=jnp.bfloat16):
    drawn = jax.random.normal(key, extent, jnp.float32) * scale
    if len(cuts) > 0:
        drawn = levels(key, extent, cuts, -0.22, 0.18) * drawn
    return jnp.clip(drawn, min=-limit, max=limit).astype(kind)


def setup_inputs(seed: int = 0) -> dict:
    arg_keys = jax.random.split(jax.random.key(seed), 10)
    return {
        "forcing": noise(arg_keys[0], (SECTORS, LEVELS, NX, CY), 1.0, 6.0, ((0, 2), (1, 4), (2, 32)), jnp.float32),
        "courant_x": jnp.clip(jax.random.uniform(arg_keys[1], (LEVELS, NX, CY), jnp.float32, -0.44921875, 0.44921875) * levels(arg_keys[1], (LEVELS, NX, CY), ((0, 4), (1, 32)), -0.4, 0.0), -0.44921875, 0.44921875).astype(jnp.bfloat16),
        "courant_y": jnp.clip(jax.random.uniform(arg_keys[2], (LEVELS, NX, CY), jnp.float32, -0.44921875, 0.44921875) * levels(arg_keys[2], (LEVELS, NX, CY), ((0, 4), (1, 32)), -0.4, 0.0), -0.44921875, 0.44921875).astype(jnp.bfloat16),
        "mass_flux": jnp.clip(0.59765625 * jax.random.uniform(arg_keys[3], (LEVELS, NX, CY), jnp.float32) ** levels(arg_keys[3], (LEVELS, NX, CY), ((0, 4), (1, 32)), -0.2, 0.2), 0.0, 0.59765625).astype(jnp.bfloat16),
        "limiter_code": set_ends(jax.random.randint(arg_keys[4], (LEVELS, NX, CY), 0, 16), jax.random.fold_in(arg_keys[4], 1), 0, 15).astype(jnp.int32),
        "seam_code": set_ends(jax.random.randint(arg_keys[5], (TILES, 2), 0, 2), jax.random.fold_in(arg_keys[5], 1), 0, 1).astype(jnp.int32),
        "level_weight": jnp.clip(jnp.exp(math.log(0.5) - 3.218876 * jax.random.uniform(arg_keys[6], (LEVELS,), jnp.float32) ** levels(arg_keys[6], (LEVELS,), ((0, 4),), -0.2, 0.2)), 0.02, 0.5),
        "sector_share": jnp.clip(jnp.exp(math.log(1.0) - 2.3025851 * jax.random.uniform(arg_keys[7], (SECTORS, NX, CY), jnp.float32) ** levels(arg_keys[7], (SECTORS, NX, CY), ((0, 2), (1, 32)), -0.2, 0.2)), 0.1, 1.0),
        "flux_cell": set_ends(jax.random.randint(arg_keys[8], (TILES * TILES, SHARE), 0, FL_DEV), jax.random.fold_in(arg_keys[8], 1), 0, FL_DEV - 1).astype(jnp.int32),
    }


def coefficients(courant, codes, bit):
    value = courant.astype(jnp.float32)
    limited = jnp.bitwise_and(jnp.right_shift(codes, bit), 1).astype(jnp.float32)
    spread = 0.5 * jnp.abs(value) * (1.0 - jnp.abs(value))
    ahead = jnp.maximum(value, 0.0) - limited * spread
    behind = jnp.minimum(value, 0.0) + limited * spread
    return ahead, behind


def vertical(adjoint, mixing):
    upper = jnp.concatenate([adjoint[1:], adjoint[-1:]], axis=0)
    return adjoint + mixing * (upper - adjoint)


def sweep_second(adjoint, courant, codes, bit):
    ahead, behind = coefficients(courant, codes, bit)
    following = jnp.concatenate([adjoint[..., 1:], adjoint[..., -1:]], axis=-1)
    previous = jnp.concatenate([adjoint[..., :1], adjoint[..., :-1]], axis=-1)
    return adjoint + ahead * (following - adjoint) + behind * (adjoint - previous)


def sweep_first(adjoint, courant, codes, bit, seam_code):
    ahead, behind = coefficients(courant, codes, bit)
    depth = adjoint.shape[0]
    width = adjoint.shape[2]
    blocks = adjoint.reshape(depth, TILES, CX, width)
    left_rim = jnp.roll(blocks[:, :, -1, :], 1, axis=1)
    right_rim = jnp.roll(blocks[:, :, 0, :], -1, axis=1)
    flip_left = (seam_code[:, 0] == 1)[None, :, None]
    flip_right = (seam_code[:, 1] == 1)[None, :, None]
    left_rim = jnp.where(flip_left, left_rim[..., ::-1], left_rim)
    right_rim = jnp.where(flip_right, right_rim[..., ::-1], right_rim)
    following = jnp.concatenate([blocks[:, :, 1:], right_rim[:, :, None]], axis=2).reshape(adjoint.shape)
    previous = jnp.concatenate([left_rim[:, :, None], blocks[:, :, :-1]], axis=2).reshape(adjoint.shape)
    return adjoint + ahead * (following - adjoint) + behind * (adjoint - previous)


def reference(forcing, courant_x, courant_y, mass_flux, limiter_code, seam_code, level_weight, sector_share, flux_cell):
    mixing = mass_flux.astype(jnp.float32)

    def one_sector(total, item):
        adjoint, share = item
        for turn_index in (1, 0):
            adjoint = vertical(adjoint, mixing)
            adjoint = sweep_second(adjoint, courant_y, limiter_code, 2 * turn_index + 1)
            adjoint = sweep_first(adjoint, courant_x, limiter_code, 2 * turn_index, seam_code)
        column_sum = jnp.einsum("l,lxy->xy", level_weight, adjoint, precision=lax.Precision.HIGHEST)
        return total + share * column_sum, adjoint

    start = jnp.zeros((NX, CY), jnp.float32)
    sensitivity, adjoint_start = lax.scan(one_sector, start, (forcing, sector_share))
    grouped = sensitivity.reshape(TILES, TILES, SHARE)
    cells = flux_cell.reshape(TILES, TILES, SHARE).transpose(1, 0, 2)
    offsets = (jnp.arange(TILES, dtype=jnp.int32) * FL_DEV)[None, :, None]
    target = (cells + offsets).astype(jnp.int32)
    flux_sensitivity = jax.ops.segment_sum(grouped.reshape(-1), target.reshape(-1), num_segments=FLUX)
    return adjoint_start, flux_sensitivity
```

```python
import functools

import jax
import jax.numpy as jnp
from jax import lax
from jax.experimental import pallas as pl
from jax.experimental.pallas import tpu as pltpu
from jax.sharding import PartitionSpec as P

SEC, LEV, ROWS, COLS = 4, 18, 40, 384
TILES = 32
OWNED = 15360
MESH = pl.DeviceIdType.MESH
ANY = pl.BlockSpec(memory_space=pl.ANY)
VMEM = pl.BlockSpec(memory_space=pltpu.VMEM)
SMEM = pl.BlockSpec(memory_space=pltpu.SMEM)
LIMIT = 56 * 1024 * 1024


def coefficients(courant, code, bit):
    size = jnp.abs(courant)
    rest = 1.0 - size
    twice = jnp.where((code & (1 << bit)) != 0, size * rest, 0.0)
    spread = 0.5 * twice
    positive = jnp.maximum(courant, 0.0)
    ahead = positive - spread
    back = (size - positive) - spread
    return ahead, back


def second_coefficients(courant, code, bit):
    ahead, back = coefficients(courant, code, bit)
    lane = lax.broadcasted_iota(jnp.int32, ahead.shape, 1)
    ahead = jnp.where(lane == COLS - 1, 0.0, ahead)
    back = jnp.where(lane == 0, 0.0, back)
    return ahead, back, 1.0 - ahead - back


def rims(left, right, flag_left, flag_right):
    both = jnp.concatenate([left, right], axis=0)
    lane = lax.broadcasted_iota(jnp.int32, (2 * SEC, 128), 1)
    parts = [
        jnp.take_along_axis(both[:, i * 128 : (i + 1) * 128], 127 - lane, axis=1)
        for i in (2, 1, 0)
    ]
    row = lax.broadcasted_iota(jnp.int32, both.shape, 0)
    flag = jnp.where(row < SEC, flag_left, flag_right)
    return jnp.where(flag == 1, jnp.concatenate(parts, axis=1), both)


def first_sweep(blocks, edges, sector, coefs):
    sub = lax.broadcasted_iota(jnp.int32, (8, COLS), 0)
    low = jnp.broadcast_to(edges[sector : sector + 1], (8, COLS))
    high = jnp.broadcast_to(edges[SEC + sector : SEC + sector + 1], (8, COLS))
    down = [low] + [pltpu.roll(b, 1, 0) for b in blocks]
    up = [pltpu.roll(b, 7, 0) for b in blocks] + [high]
    out = []
    for i, block in enumerate(blocks):
        ahead, back, centre = coefs[i]
        previous = jnp.where(sub == 0, down[i], down[i + 1])
        following = jnp.where(sub == 7, up[i + 1], up[i])
        out.append(centre * block + ahead * following + back * previous)
    return out


def first_coefficients(courant, code, bit):
    ahead, back = coefficients(courant.astype(jnp.float32), code, bit)
    centre = 1.0 - ahead - back
    return [
        (ahead[i : i + 8], back[i : i + 8], centre[i : i + 8]) for i in range(0, ROWS, 8)
    ]


def sweeps_kernel(
    seam,
    forcing,
    courant_x,
    courant_y,
    mass_flux,
    limiter,
    field,
    left0,
    right0,
    cx,
    cy,
    mf,
    code,
    halo1,
    halo0,
    passed,
    first1,
    last1,
    left1,
    right1,
    first0,
    last0,
    load_sem,
    lev_send,
    lev_recv,
    edge_send,
    edge_recv,
):
    tile, lev = lax.axis_index("tile"), lax.axis_index("lev")
    after, before = lax.rem(tile + 1, TILES), lax.rem(tile + TILES - 1, TILES)
    upper, lower = lax.rem(lev + 1, 4), lax.rem(lev + 3, 4)

    barrier = pltpu.get_barrier_semaphore()
    for device in ({"tile": after}, {"tile": before}, {"lev": upper}, {"lev": lower}):
        pl.semaphore_signal(barrier, inc=1, device_id=device, device_id_type=MESH)

    def loads(k):
        return (
            pltpu.make_async_copy(forcing.at[:, k], field.at[:, k], load_sem.at[0, k]),
            pltpu.make_async_copy(mass_flux.at[k], mf.at[k], load_sem.at[1, k]),
            pltpu.make_async_copy(courant_y.at[k], cy.at[k], load_sem.at[2, k]),
            pltpu.make_async_copy(limiter.at[k], code.at[k], load_sem.at[3, k]),
            pltpu.make_async_copy(courant_x.at[k], cx.at[k], load_sem.at[4, k]),
        )

    def start_loads(k, _):
        for copy in loads(k):
            copy.start()
        return 0

    lax.fori_loop(0, LEV, start_loads, 0)
    pl.semaphore_wait(barrier, 4)

    def level_copy(source, halo, index):
        return pltpu.make_async_remote_copy(
            source, halo, lev_send.at[index], lev_recv.at[index],
            device_id={"lev": lower}, device_id_type=MESH,
        )

    def edge_copies(k, step, first, last, left, right):
        return (
            pltpu.make_async_remote_copy(
                first.at[k], right.at[k], edge_send.at[step, 0, k], edge_recv.at[step, 0, k],
                device_id={"tile": before}, device_id_type=MESH,
            ),
            pltpu.make_async_remote_copy(
                last.at[k], left.at[k], edge_send.at[step, 1, k], edge_recv.at[step, 1, k],
                device_id={"tile": after}, device_id_type=MESH,
            ),
        )

    copy1 = level_copy(forcing.at[:, 0], halo1, 1)
    copy0 = level_copy(passed, halo0, 0)

    @pl.when(lev > 0)
    def _():
        copy1.start()

    def vertical_second(k, above, bit, step, first, last, left, right):
        for low, size in ((0, 16), (16, 16), (32, 8)):
            rows = slice(low, low + size)
            mixing = mf[k, rows, :].astype(jnp.float32)
            ahead, back, centre = second_coefficients(
                cy[k, rows, :].astype(jnp.float32), code[k, rows, :], bit
            )
            for s in range(SEC):
                value = field[s, k, rows, :]
                value = value + mixing * (above(s, rows) - value)
                value = (
                    centre * value
                    + ahead * pltpu.roll(value, COLS - 1, 1)
                    + back * pltpu.roll(value, 1, 1)
                )
                field[s, k, rows, :] = value
                if low == 0:
                    first[k, s : s + 1, :] = value[:1]
                if low == 32:
                    last[k, s : s + 1, :] = value[7:]
        for copy in edge_copies(k, step, first, last, left, right):
            copy.start()

    step1 = (3, 1, first1, last1, left1, right1)
    step0 = (1, 0, first0, last0, left0, right0)

    loads(0)[0].wait()

    def phase_a(k, _):
        loads(k + 1)[0].wait()
        for copy in loads(k)[1:4]:
            copy.wait()
        vertical_second(k, lambda s, rows: field[s, k + 1, rows, :], *step1)
        return 0

    lax.fori_loop(0, LEV - 1, phase_a, 0)

    def fill(halo, copy):
        @pl.when(lev < 3)
        def _():
            copy.wait_recv()

        @pl.when(lev == 3)
        def _():
            for s in range(SEC):
                halo[s] = field[s, LEV - 1]

    flag_left, flag_right = seam[tile, 0], seam[tile, 1]

    def phase_b(k, _):
        @pl.when(k == 9)
        def _():
            for copy in loads(LEV - 1)[1:4]:
                copy.wait()
            fill(halo1, copy1)
            vertical_second(LEV - 1, lambda s, rows: halo1[s, rows, :], *step1)

        loads(k)[4].wait()
        for copy in edge_copies(k, 1, first1, last1, left1, right1):
            copy.wait_recv()
        edges = rims(left1[k], right1[k], flag_left, flag_right)
        coefs = first_coefficients(cx[k], code[k], 2)
        for s in range(SEC):
            blocks = [field[s, k, i : i + 8, :] for i in range(0, ROWS, 8)]
            for i, block in enumerate(first_sweep(blocks, edges, s, coefs)):
                field[s, k, i * 8 : i * 8 + 8, :] = block

        @pl.when(k == 0)
        def _():
            for s in range(SEC):
                passed[s] = field[s, 0]

        @pl.when(jnp.logical_and(k == 0, lev > 0))
        def _():
            copy0.start()

        @pl.when(k > 0)
        def _():
            vertical_second(k - 1, lambda s, rows: field[s, k, rows, :], *step0)

        return 0

    lax.fori_loop(0, LEV, phase_b, 0)
    fill(halo0, copy0)
    vertical_second(LEV - 1, lambda s, rows: halo0[s, rows, :], *step0)

    def finish(k, _):
        for copy in edge_copies(k, 1, first1, last1, left1, right1):
            copy.wait_send()
        for copy in edge_copies(k, 0, first0, last0, left0, right0):
            copy.wait()
        return 0

    lax.fori_loop(0, LEV, finish, 0)

    @pl.when(lev > 0)
    def _():
        copy1.wait_send()
        copy0.wait_send()


def last_kernel(seam, weight, field, courant_x, limiter, left, right, share, out, partial, total):
    k = pl.program_id(0)
    tile = lax.axis_index("tile")
    edges = rims(left[0], right[0], seam[tile, 0], seam[tile, 1])
    coefs = first_coefficients(courant_x[0], limiter[0], 0)

    @pl.when(k == 0)
    def _():
        total[...] = jnp.zeros_like(total)

    sums = None
    for s in range(SEC):
        blocks = [field[s, 0, i : i + 8, :] for i in range(0, ROWS, 8)]
        results = first_sweep(blocks, edges, s, coefs)
        terms = []
        for i, block in enumerate(results):
            rows = slice(i * 8, i * 8 + 8)
            out[s, 0, rows, :] = block
            terms.append(share[s, rows, :] * block)
        sums = terms if sums is None else [a + b for a, b in zip(sums, terms)]
    for i, term in enumerate(sums):
        rows = slice(i * 8, i * 8 + 8)
        total[rows, :] += weight[k] * term

    @pl.when(k == LEV - 1)
    def _():
        for q in range(8):
            partial[q] = total[5 * q : 5 * q + 5, :]


def remap_kernel(
    partial, cells, out, others, outgoing, arrived, high, low,
    rs_send, rs_recv, send_sem, recv_sem,
):
    tile, lev, sec = lax.axis_index("tile"), lax.axis_index("lev"), lax.axis_index("sec")
    me = lev * 2 + sec
    mine = tile // 4

    barrier = pltpu.get_barrier_semaphore()
    own = mine == me

    def member(q):
        return {"tile": tile, "lev": q // 2, "sec": lax.rem(q, 2)}

    for p in range(1, 8):
        pl.semaphore_signal(
            barrier, inc=1, device_id=member(lax.rem(me + p, 8)), device_id_type=MESH
        )

    def greet(t, _):
        @pl.when(jnp.logical_not(jnp.logical_and(own, t == tile)))
        def _():
            pl.semaphore_signal(
                barrier, inc=1,
                device_id={"tile": t, "lev": mine // 2, "sec": lax.rem(mine, 2)},
                device_id_type=MESH,
            )
        return 0

    lax.fori_loop(0, TILES, greet, 0)

    @pl.when(own)
    def _():
        pl.semaphore_wait(barrier, 7 + 31)

    @pl.when(jnp.logical_not(own))
    def _():
        pl.semaphore_wait(barrier, 7 + 32)

    def reduce_copy(p):
        peer = lax.rem(me + p, 8)
        return pltpu.make_async_remote_copy(
            partial.at[peer], others.at[p - 1], rs_send.at[p - 1], rs_recv.at[p - 1],
            device_id=member(peer), device_id_type=MESH,
        )

    for p in range(1, 8):
        reduce_copy(p).start()

    slot = lax.broadcasted_iota(jnp.int32, (128, 512), 0)

    def one_hot(t, _):
        cell = cells[t]
        high[t] = jnp.where(slot == (cell >> 7), 1.0, 0.0).astype(jnp.bfloat16)
        low[t] = jnp.where(slot == (cell & 127), 1.0, 0.0).astype(jnp.bfloat16)
        return 0

    lax.fori_loop(0, TILES, one_hot, 0)

    summed = partial[me]
    for p in range(1, 8):
        reduce_copy(p).wait_recv()
        summed = summed + others[p - 1]
    for r in range(4):
        pair = jnp.concatenate([summed[r : r + 1], summed[r + 1 : r + 2]], axis=1)
        if r:
            pair = pltpu.roll(pair, 768 - 96 * r, 1)
        outgoing[r] = pair[:, :512]

    def send_copy(i):
        owner = me * 4 + i // 8
        return pltpu.make_async_remote_copy(
            outgoing.at[i // 8], arrived.at[tile], send_sem.at[i], recv_sem.at[tile],
            device_id={"tile": owner, "lev": lax.rem(i, 8) // 2, "sec": lax.rem(i, 2)},
            device_id_type=MESH,
        )

    def is_self(i):
        return jnp.logical_and(me * 4 + i // 8 == tile, lax.rem(i, 8) == me)

    def send(i, _):
        @pl.when(jnp.logical_not(is_self(i)))
        def _():
            send_copy(i).start()

        @pl.when(is_self(i))
        def _():
            pltpu.make_async_copy(
                outgoing.at[i // 8], arrived.at[tile], recv_sem.at[tile]
            ).start()
        return 0

    lax.fori_loop(0, TILES, send, 0)

    def accumulate(t, total):
        pltpu.make_async_copy(arrived.at[t], arrived.at[t], recv_sem.at[t]).wait()
        value = arrived[t]
        for _ in range(3):
            piece = value.astype(jnp.bfloat16)
            value = value - piece.astype(jnp.float32)
            spread = high[t] * jnp.broadcast_to(piece, (128, 512))
            total = total + lax.dot_general(
                spread, low[t], (((1,), (1,)), ((), ())),
                preferred_element_type=jnp.float32,
            )
        return total

    total = lax.fori_loop(0, TILES, accumulate, jnp.zeros((128, 128), jnp.float32))
    out[...] = total[: OWNED // 128]

    for p in range(1, 8):
        reduce_copy(p).wait_send()

    def finish(i, _):
        @pl.when(jnp.logical_not(is_self(i)))
        def _():
            send_copy(i).wait_send()
        return 0

    lax.fori_loop(0, TILES, finish, 0)


def shards(
    forcing, courant_x, courant_y, mass_flux, limiter_code, seam_code, level_weight,
    sector_share, flux_cell,
):
    f32, bf16, i32 = jnp.float32, jnp.bfloat16, jnp.int32
    shape = jax.ShapeDtypeStruct
    dma = pltpu.SemaphoreType.DMA
    edge = (LEV, SEC, COLS)
    plane = (SEC, ROWS, COLS)
    grid3 = (LEV, ROWS, COLS)
    field, left0, right0 = pl.pallas_call(
        sweeps_kernel,
        out_shape=(shape(forcing.shape, f32), shape(edge, f32), shape(edge, f32)),
        in_specs=[SMEM] + [ANY] * 5,
        out_specs=[VMEM] * 3,
        scratch_shapes=[
            pltpu.VMEM(grid3, bf16),
            pltpu.VMEM(grid3, bf16),
            pltpu.VMEM(grid3, bf16),
            pltpu.VMEM(grid3, i32),
            pltpu.VMEM(plane, f32),
            pltpu.VMEM(plane, f32),
            pltpu.VMEM(plane, f32),
        ]
        + [pltpu.VMEM(edge, f32)] * 6
        + [dma((5, LEV)), dma((2,)), dma((2,)), dma((2, 2, LEV)), dma((2, 2, LEV))],
        compiler_params=pltpu.CompilerParams(
            collective_id=0, has_side_effects=True, vmem_limit_bytes=LIMIT
        ),
        name="sweeps",
    )(seam_code, forcing, courant_x, courant_y, mass_flux, limiter_code)

    level = pl.BlockSpec((SEC, 1, ROWS, COLS), lambda k: (0, k, 0, 0))
    one = pl.BlockSpec((1, ROWS, COLS), lambda k: (k, 0, 0))
    rim = pl.BlockSpec((1, SEC, COLS), lambda k: (k, 0, 0))
    adjoint, partial = pl.pallas_call(
        last_kernel,
        out_shape=(shape(forcing.shape, f32), shape((8, 5, COLS), f32)),
        grid=(LEV,),
        in_specs=[
            SMEM, SMEM, level, one, one, rim, rim,
            pl.BlockSpec((SEC, ROWS, COLS), lambda k: (0, 0, 0)),
        ],
        out_specs=[level, pl.BlockSpec((8, 5, COLS), lambda k: (0, 0, 0))],
        scratch_shapes=[pltpu.VMEM((ROWS, COLS), f32)],
        compiler_params=pltpu.CompilerParams(vmem_limit_bytes=LIMIT),
        name="last_sweep",
    )(seam_code, level_weight, field, courant_x, limiter_code, left0, right0, sector_share)

    cells = jnp.pad(flux_cell, ((0, 0), (0, 32)), constant_values=-1)[:, None, :]
    flux = pl.pallas_call(
        remap_kernel,
        out_shape=shape((OWNED // 128, 128), f32),
        in_specs=[VMEM, VMEM],
        out_specs=VMEM,
        scratch_shapes=[
            pltpu.VMEM((7, 5, COLS), f32),
            pltpu.VMEM((4, 1, 512), f32),
            pltpu.VMEM((TILES, 1, 512), f32),
            pltpu.VMEM((TILES, 128, 512), bf16),
            pltpu.VMEM((TILES, 128, 512), bf16),
            dma((7,)), dma((7,)), dma((TILES,)), dma((TILES,)),
        ],
        compiler_params=pltpu.CompilerParams(
            collective_id=1, has_side_effects=True, vmem_limit_bytes=LIMIT
        ),
        name="remap",
    )(partial, cells)
    return adjoint, flux.reshape(-1)


def solution(mesh):
    placed = (
        P("sec", "lev", "tile", None),
        P("lev", "tile", None),
        P("lev", "tile", None),
        P("lev", "tile", None),
        P("lev", "tile", None),
        P(),
        P("lev"),
        P("sec", "tile", None),
        P("tile", None),
    )
    return jax.shard_map(
        shards,
        mesh=mesh,
        in_specs=placed,
        out_specs=(P("sec", "lev", "tile", None), P("tile")),
        check_vma=False,
    )
```

```python
import functools

import jax
import jax.numpy as jnp
from jax import lax
from jax.experimental import pallas as pl
from jax.experimental.pallas import tpu as pltpu
from jax.sharding import PartitionSpec as P

SEC, LEV, ROWS, COLS = 4, 18, 40, 384
TILES = 32
OWNED = 15360
MESH = pl.DeviceIdType.MESH
HBM = pl.BlockSpec(memory_space=pltpu.HBM)
VMEM = pl.BlockSpec(memory_space=pltpu.VMEM)
SMEM = pl.BlockSpec(memory_space=pltpu.SMEM)
MIB = 1024 * 1024
LIMIT_FIRST = 32
LIMIT_SECOND = 18


def coefficients(courant, code, bit):
    size = jnp.abs(courant)
    rest = 1.0 - size
    twice = jnp.where((code & (1 << bit)) != 0, size * rest, 0.0)
    spread = 0.5 * twice
    positive = jnp.maximum(courant, 0.0)
    ahead = positive - spread
    back = (size - positive) - spread
    return ahead, back


def second_coefficients(courant, code, bit):
    ahead, back = coefficients(courant, code, bit)
    lane = lax.broadcasted_iota(jnp.int32, ahead.shape, 1)
    ahead = jnp.where(lane == COLS - 1, 0.0, ahead)
    back = jnp.where(lane == 0, 0.0, back)
    return ahead, back, 1.0 - ahead - back


def rims(left, right, flag_left, flag_right):
    both = jnp.concatenate([left, right], axis=0)
    lane = lax.broadcasted_iota(jnp.int32, (2 * SEC, 128), 1)
    parts = [
        jnp.take_along_axis(both[:, i * 128 : (i + 1) * 128], 127 - lane, axis=1)
        for i in (2, 1, 0)
    ]
    row = lax.broadcasted_iota(jnp.int32, both.shape, 0)
    flag = jnp.where(row < SEC, flag_left, flag_right)
    return jnp.where(flag == 1, jnp.concatenate(parts, axis=1), both)


def first_sweep(blocks, edges, sector, coefs):
    sub = lax.broadcasted_iota(jnp.int32, (8, COLS), 0)
    low = jnp.broadcast_to(edges[sector : sector + 1], (8, COLS))
    high = jnp.broadcast_to(edges[SEC + sector : SEC + sector + 1], (8, COLS))
    down = [low] + [pltpu.roll(b, 1, 0) for b in blocks]
    up = [pltpu.roll(b, 7, 0) for b in blocks] + [high]
    out = []
    for i, block in enumerate(blocks):
        ahead, back, centre = coefs[i]
        previous = jnp.where(sub == 0, down[i], down[i + 1])
        following = jnp.where(sub == 7, up[i + 1], up[i])
        out.append(centre * block + ahead * following + back * previous)
    return out


def first_coefficients(courant, code, bit):
    ahead, back = coefficients(courant.astype(jnp.float32), code, bit)
    centre = 1.0 - ahead - back
    return [
        (ahead[i : i + 8], back[i : i + 8], centre[i : i + 8]) for i in range(0, ROWS, 8)
    ]


def adjoint_kernel(
    seam_code,
    level_weight,
    forcing,
    courant_x,
    courant_y,
    mass_flux,
    limiter,
    sector_share,
    flux_cell,
    out,
    arrived,
    high,
    low,
    seam,
    weight,
    field,
    swept,
    cx,
    cy,
    mf,
    code,
    share,
    cells,
    padded,
    halo1,
    halo0,
    first1,
    last1,
    left1,
    right1,
    first0,
    last0,
    left0,
    right0,
    total,
    partial,
    others,
    outgoing,
    load_sem,
    extra_sem,
    lev_send,
    lev_recv,
    edge_send,
    edge_recv,
    rs_send,
    rs_recv,
    send_sem,
    recv_sem,
):
    tile, lev, sec = lax.axis_index("tile"), lax.axis_index("lev"), lax.axis_index("sec")
    after, before = lax.rem(tile + 1, TILES), lax.rem(tile + TILES - 1, TILES)
    upper, lower = lax.rem(lev + 1, 4), lax.rem(lev + 3, 4)
    me = lev * 2 + sec
    mine = tile // 4
    own = mine == me

    def member(q):
        return {"tile": tile, "lev": q // 2, "sec": lax.rem(q, 2)}

    def loads(k):
        return (
            pltpu.make_async_copy(forcing.at[:, k], field.at[:, k], load_sem.at[0, k]),
            pltpu.make_async_copy(mass_flux.at[k], mf.at[k], load_sem.at[1, k]),
            pltpu.make_async_copy(courant_y.at[k], cy.at[k], load_sem.at[2, k]),
            pltpu.make_async_copy(limiter.at[k], code.at[k], load_sem.at[3, k]),
            pltpu.make_async_copy(courant_x.at[k], cx.at[k], load_sem.at[4, k]),
        )

    def start_loads(k, _):
        for copy in loads(k):
            copy.start()
        return 0

    share_copy = pltpu.make_async_copy(sector_share, share, extra_sem.at[0])
    cells_copy = pltpu.make_async_copy(flux_cell, cells, extra_sem.at[1])
    seam_copy = pltpu.make_async_copy(seam_code, seam, extra_sem.at[2])
    weight_copy = pltpu.make_async_copy(level_weight, weight, extra_sem.at[3])

    barrier = pltpu.get_barrier_semaphore()
    for device in ({"tile": after}, {"tile": before}, {"lev": upper}, {"lev": lower}):
        pl.semaphore_signal(barrier, inc=1, device_id=device, device_id_type=MESH)
    for p in range(1, 8):
        pl.semaphore_signal(
            barrier, inc=1, device_id=member(lax.rem(me + p, 8)), device_id_type=MESH
        )

    def greet(t, _):
        @pl.when(jnp.logical_not(jnp.logical_and(own, t == tile)))
        def _():
            pl.semaphore_signal(
                barrier, inc=1,
                device_id={"tile": t, "lev": mine // 2, "sec": lax.rem(mine, 2)},
                device_id_type=MESH,
            )
        return 0

    lax.fori_loop(0, TILES, greet, 0)
    lax.fori_loop(0, LEV, start_loads, 0)
    for copy in (share_copy, cells_copy, seam_copy, weight_copy):
        copy.start()

    @pl.when(own)
    def _():
        pl.semaphore_wait(barrier, 4 + 7 + 31)

    @pl.when(jnp.logical_not(own))
    def _():
        pl.semaphore_wait(barrier, 4 + 7 + 32)

    def level_copy(source, halo, index):
        return pltpu.make_async_remote_copy(
            source, halo, lev_send.at[index], lev_recv.at[index],
            device_id={"lev": lower}, device_id_type=MESH,
        )

    def edge_copies(k, step, first, last, left, right):
        return (
            pltpu.make_async_remote_copy(
                first.at[k], right.at[k], edge_send.at[step, 0, k], edge_recv.at[step, 0, k],
                device_id={"tile": before}, device_id_type=MESH,
            ),
            pltpu.make_async_remote_copy(
                last.at[k], left.at[k], edge_send.at[step, 1, k], edge_recv.at[step, 1, k],
                device_id={"tile": after}, device_id_type=MESH,
            ),
        )

    copy1 = level_copy(forcing.at[:, 0], halo1, 1)
    copy0 = level_copy(field.at[:, 0], halo0, 0)

    @pl.when(lev > 0)
    def _():
        copy1.start()

    def vertical_second(k, above, bit, step, first, last, left, right):
        for start, size in ((0, 16), (16, 16), (32, 8)):
            rows = slice(start, start + size)
            mixing = mf[k, rows, :].astype(jnp.float32)
            ahead, back, centre = second_coefficients(
                cy[k, rows, :].astype(jnp.float32), code[k, rows, :], bit
            )
            for s in range(SEC):
                value = field[s, k, rows, :]
                value = value + mixing * (above(s, rows) - value)
                value = (
                    centre * value
                    + ahead * pltpu.roll(value, COLS - 1, 1)
                    + back * pltpu.roll(value, 1, 1)
                )
                swept[s, k, rows, :] = value
                if start == 0:
                    first[k, s : s + 1, :] = value[:1]
                if start == 32:
                    last[k, s : s + 1, :] = value[7:]
        for copy in edge_copies(k, step, first, last, left, right):
            copy.start()

    edges1 = (first1, last1, left1, right1)
    edges0 = (first0, last0, left0, right0)
    step1 = (3, 1) + edges1
    step0 = (1, 0) + edges0

    loads(0)[0].wait()

    def phase_a(k, _):
        loads(k + 1)[0].wait()
        for copy in loads(k)[1:4]:
            copy.wait()
        vertical_second(k, lambda s, rows: field[s, k + 1, rows, :], *step1)
        return 0

    lax.fori_loop(0, LEV - 1, phase_a, 0)

    def fill(halo, copy):
        @pl.when(lev < 3)
        def _():
            copy.wait_recv()

        @pl.when(lev == 3)
        def _():
            for s in range(SEC):
                halo[s] = field[s, LEV - 1]

    seam_copy.wait()
    flag_left, flag_right = seam[0, tile], seam[1, tile]

    def first_dimension(k, step, edges, bit, target):
        for copy in edge_copies(k, step, *edges):
            copy.wait_recv()
        rim = rims(edges[2][k], edges[3][k], flag_left, flag_right)
        coefs = first_coefficients(cx[k], code[k], bit)
        results = []
        for s in range(SEC):
            blocks = [swept[s, k, i : i + 8, :] for i in range(0, ROWS, 8)]
            blocks = first_sweep(blocks, rim, s, coefs)
            for i, block in enumerate(blocks):
                target[s, k, i * 8 : i * 8 + 8, :] = block
            results.append(blocks)
        return results

    loads(0)[4].wait()
    first_dimension(0, 1, edges1, 2, field)

    @pl.when(lev > 0)
    def _():
        copy0.start()

    def phase_b(k, _):
        @pl.when(k == 8)
        def _():
            for copy in loads(LEV - 1)[1:4]:
                copy.wait()
            fill(halo1, copy1)
            vertical_second(LEV - 1, lambda s, rows: halo1[s, rows, :], *step1)

        loads(k + 1)[4].wait()
        first_dimension(k + 1, 1, edges1, 2, field)
        vertical_second(k, lambda s, rows: field[s, k + 1, rows, :], *step0)
        return 0

    lax.fori_loop(0, LEV - 1, phase_b, 0)

    share_copy.wait()
    weight_copy.wait()
    total[...] = jnp.zeros_like(total)

    def phase_c(k, _):
        @pl.when(k == 8)
        def _():
            fill(halo0, copy0)
            vertical_second(LEV - 1, lambda s, rows: halo0[s, rows, :], *step0)

        results = first_dimension(k, 0, edges0, 0, out)
        for i in range(ROWS // 8):
            rows = slice(i * 8, i * 8 + 8)
            term = share[0, rows, :] * results[0][i]
            for s in range(1, SEC):
                term = term + share[s, rows, :] * results[s][i]
            total[rows, :] += weight[k] * term
        return 0

    lax.fori_loop(0, LEV, phase_c, 0)

    for q in range(8):
        partial[q] = total[5 * q : 5 * q + 5, :]

    def reduce_copy(p):
        return pltpu.make_async_remote_copy(
            partial.at[lax.rem(me + p, 8)], others.at[p - 1],
            rs_send.at[p - 1], rs_recv.at[p - 1],
            device_id=member(lax.rem(me + p, 8)), device_id_type=MESH,
        )

    for p in range(1, 8):
        reduce_copy(p).start()

    cells_copy.wait()
    padded[...] = jnp.concatenate(
        [cells[...], jnp.full((TILES, 32), -1, jnp.int32)], axis=1
    )
    slot = lax.broadcasted_iota(jnp.int32, (128, 512), 0)

    def one_hot(t, _):
        cell = padded[pl.ds(t, 1), :]
        high[t] = jnp.where(slot == (cell >> 7), 1.0, 0.0).astype(jnp.bfloat16)
        low[t] = jnp.where(slot == (cell & 127), 1.0, 0.0).astype(jnp.bfloat16)
        return 0

    lax.fori_loop(0, TILES, one_hot, 0)

    summed = partial[me]
    for p in range(1, 8):
        reduce_copy(p).wait_recv()
        summed = summed + others[p - 1]
    for r in range(4):
        pair = jnp.concatenate([summed[r : r + 1], summed[r + 1 : r + 2]], axis=1)
        if r:
            pair = pltpu.roll(pair, 768 - 96 * r, 1)
        outgoing[r] = pair[:, :512]

    def send_copy(i):
        return pltpu.make_async_remote_copy(
            outgoing.at[i // 8], arrived.at[tile], send_sem.at[i], recv_sem.at[tile],
            device_id={
                "tile": me * 4 + i // 8, "lev": lax.rem(i, 8) // 2, "sec": lax.rem(i, 2),
            },
            device_id_type=MESH,
        )

    def is_self(i):
        return jnp.logical_and(me * 4 + i // 8 == tile, lax.rem(i, 8) == me)

    def send(i, _):
        @pl.when(jnp.logical_not(is_self(i)))
        def _():
            send_copy(i).start()

        @pl.when(is_self(i))
        def _():
            pltpu.make_async_copy(
                outgoing.at[i // 8], arrived.at[tile], recv_sem.at[tile]
            ).start()
        return 0

    lax.fori_loop(0, TILES, send, 0)

    def finish_edges(k, _):
        for copy in edge_copies(k, 1, *edges1) + edge_copies(k, 0, *edges0):
            copy.wait_send()
        return 0

    lax.fori_loop(0, LEV, finish_edges, 0)

    @pl.when(lev > 0)
    def _():
        copy1.wait_send()
        copy0.wait_send()

    for p in range(1, 8):
        reduce_copy(p).wait_send()

    def finish(i, _):
        @pl.when(jnp.logical_not(is_self(i)))
        def _():
            send_copy(i).wait_send()

        pltpu.make_async_copy(arrived.at[i], arrived.at[i], recv_sem.at[i]).wait()
        return 0

    lax.fori_loop(0, TILES, finish, 0)


def remap_kernel(adjoint, arrived, high, low, adjoint_out, flux, sem):
    copy = pltpu.make_async_copy(adjoint, adjoint_out, sem)
    copy.start()

    def accumulate(t, total):
        value = arrived[t]
        for _ in range(3):
            piece = value.astype(jnp.bfloat16)
            value = value - piece.astype(jnp.float32)
            spread = high[t] * jnp.broadcast_to(piece, (128, 512))
            total = total + lax.dot_general(
                spread, low[t], (((1,), (1,)), ((), ())),
                preferred_element_type=jnp.float32,
            )
        return total

    total = lax.fori_loop(
        0, TILES, accumulate, jnp.zeros((128, 128), jnp.float32), unroll=4
    )
    flux[...] = total[: OWNED // 128]
    copy.wait()


def shards(
    forcing, courant_x, courant_y, mass_flux, limiter_code, seam_code, level_weight,
    sector_share, flux_cell,
):
    f32, bf16, i32 = jnp.float32, jnp.bfloat16, jnp.int32
    shape = jax.ShapeDtypeStruct
    dma = pltpu.SemaphoreType.DMA
    edge = pltpu.VMEM((LEV, SEC, COLS), f32)
    plane = pltpu.VMEM((SEC, ROWS, COLS), f32)
    levels = (LEV, ROWS, COLS)
    passed = pl.pallas_call(
        adjoint_kernel,
        out_shape=(
            shape(forcing.shape, f32),
            shape((TILES, 1, 512), f32),
            shape((TILES, 128, 512), bf16),
            shape((TILES, 128, 512), bf16),
        ),
        in_specs=[HBM] * 9,
        out_specs=[VMEM] * 4,
        scratch_shapes=[pltpu.SMEM((2, TILES), i32), pltpu.SMEM((LEV,), f32)]
        + [pltpu.VMEM(forcing.shape, f32)] * 2
        + [pltpu.VMEM(levels, bf16)] * 3
        + [pltpu.VMEM(levels, i32)]
        + [plane]
        + [pltpu.VMEM((TILES, 480), i32), pltpu.VMEM((TILES, 512), i32)]
        + [plane] * 2
        + [edge] * 8
        + [
            pltpu.VMEM((ROWS, COLS), f32),
            pltpu.VMEM((8, 5, COLS), f32),
            pltpu.VMEM((7, 5, COLS), f32),
            pltpu.VMEM((4, 1, 512), f32),
        ]
        + [dma((5, LEV)), dma((4,)), dma((2,)), dma((2,)), dma((2, 2, LEV)), dma((2, 2, LEV))]
        + [dma((7,)), dma((7,)), dma((TILES,)), dma((TILES,))],
        compiler_params=pltpu.CompilerParams(
            collective_id=0, has_side_effects=True, vmem_limit_bytes=LIMIT_FIRST * MIB
        ),
        name="adjoint",
    )(
        *(
            pltpu.with_memory_space_constraint(x, pltpu.HBM)
            for x in (
                seam_code.T, level_weight, forcing, courant_x, courant_y, mass_flux,
                limiter_code, sector_share, flux_cell,
            )
        ),
    )
    adjoint, flux = pl.pallas_call(
        remap_kernel,
        out_shape=(shape(forcing.shape, f32), shape((OWNED // 128, 128), f32)),
        in_specs=[VMEM] * 4,
        out_specs=[HBM, VMEM],
        scratch_shapes=[dma],
        compiler_params=pltpu.CompilerParams(vmem_limit_bytes=LIMIT_SECOND * MIB),
        name="remap",
    )(*passed)
    return adjoint, flux.reshape(-1)


def solution(mesh):
    placed = (
        P("sec", "lev", "tile", None),
        P("lev", "tile", None),
        P("lev", "tile", None),
        P("lev", "tile", None),
        P("lev", "tile", None),
        P(),
        P("lev"),
        P("sec", "tile", None),
        P("tile", None),
    )
    return jax.shard_map(
        shards,
        mesh=mesh,
        in_specs=placed,
        out_specs=(P("sec", "lev", "tile", None), P("tile")),
        check_vma=False,
    )
```

```python
import functools

import jax
import jax.numpy as jnp
from jax import lax
from jax.experimental import pallas as pl
from jax.experimental.pallas import tpu as pltpu
from jax.sharding import PartitionSpec as P

SEC, LEV, ROWS, COLS = 4, 18, 40, 384
TILES = 32
OWNED = 15360
MESH = pl.DeviceIdType.MESH
HBM = pl.BlockSpec(memory_space=pltpu.HBM)
VMEM = pl.BlockSpec(memory_space=pltpu.VMEM)
SMEM = pl.BlockSpec(memory_space=pltpu.SMEM)
MIB = 1024 * 1024
LIMIT_FIRST = 40
LIMIT_SECOND = 8
MEET_AT, HALO1_AT, TAIL_AT, HALO0_AT = 2, 12, 8, 14


def coefficients(courant, code, bit):
    size = jnp.abs(courant)
    rest = 1.0 - size
    twice = jnp.where((code & (1 << bit)) != 0, size * rest, 0.0)
    spread = 0.5 * twice
    positive = jnp.maximum(courant, 0.0)
    ahead = positive - spread
    back = (size - positive) - spread
    return ahead, back


def second_coefficients(courant, code, bit):
    ahead, back = coefficients(courant, code, bit)
    lane = lax.broadcasted_iota(jnp.int32, ahead.shape, 1)
    ahead = jnp.where(lane == COLS - 1, 0.0, ahead)
    back = jnp.where(lane == 0, 0.0, back)
    return ahead, back, 1.0 - ahead - back


def rims(left, right, flag_left, flag_right):
    both = jnp.concatenate([left, right], axis=0)
    lane = lax.broadcasted_iota(jnp.int32, (2 * SEC, 128), 1)
    parts = [
        jnp.take_along_axis(both[:, i * 128 : (i + 1) * 128], 127 - lane, axis=1)
        for i in (2, 1, 0)
    ]
    row = lax.broadcasted_iota(jnp.int32, both.shape, 0)
    flag = jnp.where(row < SEC, flag_left, flag_right)
    return jnp.where(flag == 1, jnp.concatenate(parts, axis=1), both)


def first_sweep(blocks, edges, sector, coefs):
    sub = lax.broadcasted_iota(jnp.int32, (8, COLS), 0)
    low = jnp.broadcast_to(edges[sector : sector + 1], (8, COLS))
    high = jnp.broadcast_to(edges[SEC + sector : SEC + sector + 1], (8, COLS))
    down = [low] + [pltpu.roll(b, 1, 0) for b in blocks]
    up = [pltpu.roll(b, 7, 0) for b in blocks] + [high]
    out = []
    for i, block in enumerate(blocks):
        ahead, back, centre = coefs[i]
        previous = jnp.where(sub == 0, down[i], down[i + 1])
        following = jnp.where(sub == 7, up[i + 1], up[i])
        out.append(centre * block + ahead * following + back * previous)
    return out


def first_coefficients(courant, code, bit):
    ahead, back = coefficients(courant.astype(jnp.float32), code, bit)
    centre = 1.0 - ahead - back
    return [
        (ahead[i : i + 8], back[i : i + 8], centre[i : i + 8]) for i in range(0, ROWS, 8)
    ]


def adjoint_kernel(
    seam_code,
    level_weight,
    forcing,
    courant_x,
    courant_y,
    mass_flux,
    limiter,
    sector_share,
    flux_cell,
    out,
    flux,
    seam,
    weight,
    field,
    swept,
    cx,
    cy,
    mf,
    code,
    share,
    cells,
    padded,
    halo1,
    halo0,
    first1,
    last1,
    left1,
    right1,
    first0,
    last0,
    left0,
    right0,
    total,
    partial,
    others,
    outgoing,
    arrived,
    high,
    low,
    load_sem,
    extra_sem,
    lev_send,
    lev_recv,
    edge_send,
    edge_recv,
    rs_send,
    rs_recv,
    send_sem,
    recv_sem,
    ready,
):
    tile, lev, sec = lax.axis_index("tile"), lax.axis_index("lev"), lax.axis_index("sec")
    after, before = lax.rem(tile + 1, TILES), lax.rem(tile + TILES - 1, TILES)
    lower = lax.rem(lev + 3, 4)
    me = lev * 2 + sec

    def member(q):
        return {"tile": tile, "lev": q // 2, "sec": lax.rem(q, 2)}

    def loads(k):
        return (
            pltpu.make_async_copy(forcing.at[:, k], field.at[:, k], load_sem.at[0, k]),
            pltpu.make_async_copy(mass_flux.at[k], mf.at[k], load_sem.at[1, k]),
            pltpu.make_async_copy(courant_y.at[k], cy.at[k], load_sem.at[2, k]),
            pltpu.make_async_copy(limiter.at[k], code.at[k], load_sem.at[3, k]),
            pltpu.make_async_copy(courant_x.at[k], cx.at[k], load_sem.at[4, k]),
        )

    def start_loads(k, _):
        for copy in loads(k):
            copy.start()
        return 0

    share_copy = pltpu.make_async_copy(sector_share, share, extra_sem.at[0])
    cells_copy = pltpu.make_async_copy(flux_cell, cells, extra_sem.at[1])
    seam_copy = pltpu.make_async_copy(seam_code, seam, extra_sem.at[2])
    weight_copy = pltpu.make_async_copy(level_weight, weight, extra_sem.at[3])

    barrier = pltpu.get_barrier_semaphore()
    along_z, along_x, core = tile // 8, lax.rem(tile // 2, 4), lax.rem(tile, 2)

    def tile_at(z, x, c):
        return {"tile": (lax.rem(z, 4) * 4 + lax.rem(x, 4)) * 2 + lax.rem(c, 2)}

    beside_z = [tile_at(along_z + i, along_x, core) for i in (1, 3)]
    beside_x = [tile_at(along_z, along_x + i, core) for i in (1, 3)]
    near = [{"tile": after}, {"tile": before}] + beside_z + beside_x
    near += [member(lax.rem(me + p, 8)) for p in range(1, 8)]
    for device in near:
        pl.semaphore_signal(barrier, inc=1, device_id=device, device_id_type=MESH)

    stages = (beside_z, beside_z, beside_x, beside_x, [tile_at(along_z, along_x, core + 1)])

    def tell(i):
        for device in stages[i]:
            pl.semaphore_signal(ready.at[i], inc=1, device_id=device, device_id_type=MESH)

    def hear(i):
        pl.semaphore_wait(ready.at[i], len(stages[i]))

    lax.fori_loop(0, LEV, start_loads, 0)
    for copy in (share_copy, cells_copy, seam_copy, weight_copy):
        copy.start()

    def level_copy(source, halo, index):
        return pltpu.make_async_remote_copy(
            source, halo, lev_send.at[index], lev_recv.at[index],
            device_id={"lev": lower}, device_id_type=MESH,
        )

    def edge_copies(k, step, first, last, left, right):
        return (
            pltpu.make_async_remote_copy(
                first.at[k], right.at[k], edge_send.at[step, 0, k], edge_recv.at[step, 0, k],
                device_id={"tile": before}, device_id_type=MESH,
            ),
            pltpu.make_async_remote_copy(
                last.at[k], left.at[k], edge_send.at[step, 1, k], edge_recv.at[step, 1, k],
                device_id={"tile": after}, device_id_type=MESH,
            ),
        )

    copy1 = level_copy(forcing.at[:, 0], halo1, 1)
    copy0 = level_copy(field.at[:, 0], halo0, 0)

    def meet():
        pl.semaphore_wait(barrier, len(near))
        tell(0)

        @pl.when(lev > 0)
        def _():
            copy1.start()

    def vertical_second(k, above, bit, step, first, last, left, right):
        for start, size in ((0, 16), (16, 16), (32, 8)):
            rows = slice(start, start + size)
            mixing = mf[k, rows, :].astype(jnp.float32)
            ahead, back, centre = second_coefficients(
                cy[k, rows, :].astype(jnp.float32), code[k, rows, :], bit
            )
            for s in range(SEC):
                value = field[s, k, rows, :]
                value = value + mixing * (above(s, rows) - value)
                value = (
                    centre * value
                    + ahead * pltpu.roll(value, COLS - 1, 1)
                    + back * pltpu.roll(value, 1, 1)
                )
                swept[s, k, rows, :] = value
                if start == 0:
                    first[k, s : s + 1, :] = value[:1]
                if start == 32:
                    last[k, s : s + 1, :] = value[7:]

    def send_edges(k, step, edges):
        for copy in edge_copies(k, step, *edges):
            copy.start()

    edges1 = (first1, last1, left1, right1)
    edges0 = (first0, last0, left0, right0)
    step1 = (3, 1) + edges1
    step0 = (1, 0) + edges0

    loads(0)[0].wait()

    def phase_a(k, _):
        loads(k + 1)[0].wait()
        for copy in loads(k)[1:4]:
            copy.wait()
        vertical_second(k, lambda s, rows: field[s, k + 1, rows, :], *step1)

        @pl.when(k == MEET_AT)
        def _():
            meet()

            def earlier(j, _):
                send_edges(j, 1, edges1)
                return 0

            lax.fori_loop(0, MEET_AT, earlier, 0)

        @pl.when(k >= MEET_AT)
        def _():
            send_edges(k, 1, edges1)

        return 0

    lax.fori_loop(0, LEV - 1, phase_a, 0)

    def fill(halo, copy):
        @pl.when(lev < 3)
        def _():
            copy.wait_recv()

        @pl.when(lev == 3)
        def _():
            for s in range(SEC):
                halo[s] = field[s, LEV - 1]

    seam_copy.wait()
    flag_left, flag_right = seam[0, tile], seam[1, tile]

    def first_dimension(k, step, edges, bit, target):
        for copy in edge_copies(k, step, *edges):
            copy.wait_recv()
        rim = rims(edges[2][k], edges[3][k], flag_left, flag_right)
        coefs = first_coefficients(cx[k], code[k], bit)
        results = []
        for s in range(SEC):
            blocks = [swept[s, k, i : i + 8, :] for i in range(0, ROWS, 8)]
            blocks = first_sweep(blocks, rim, s, coefs)
            for i, block in enumerate(blocks):
                target[s, k, i * 8 : i * 8 + 8, :] = block
            results.append(blocks)
        return results

    loads(0)[4].wait()
    first_dimension(0, 1, edges1, 2, field)

    @pl.when(lev > 0)
    def _():
        copy0.start()

    hear(0)
    tell(1)

    def phase_b(k, _):
        for stage, turn in ((1, 5), (2, 11)):

            @pl.when(k == turn)
            def _():
                hear(stage)
                tell(stage + 1)

        @pl.when(k == HALO1_AT)
        def _():
            for copy in loads(LEV - 1)[1:4]:
                copy.wait()
            fill(halo1, copy1)
            vertical_second(LEV - 1, lambda s, rows: halo1[s, rows, :], *step1)
            send_edges(LEV - 1, 1, edges1)

        loads(k + 1)[4].wait()
        first_dimension(k + 1, 1, edges1, 2, field)
        vertical_second(k, lambda s, rows: field[s, k + 1, rows, :], *step0)
        send_edges(k, 0, edges0)
        return 0

    lax.fori_loop(0, LEV - 2, phase_b, 0)
    loads(LEV - 1)[4].wait()
    share_copy.wait()
    weight_copy.wait()
    total[...] = jnp.zeros_like(total)

    def phase_c(k, _):
        @pl.when(k == 2)
        def _():
            hear(3)
            tell(4)

        @pl.when(k == TAIL_AT)
        def _():
            first_dimension(LEV - 1, 1, edges1, 2, field)
            vertical_second(LEV - 2, lambda s, rows: field[s, LEV - 1, rows, :], *step0)
            send_edges(LEV - 2, 0, edges0)

        @pl.when(k == HALO0_AT)
        def _():
            fill(halo0, copy0)
            vertical_second(LEV - 1, lambda s, rows: halo0[s, rows, :], *step0)
            send_edges(LEV - 1, 0, edges0)

        results = first_dimension(k, 0, edges0, 0, out)
        for i in range(ROWS // 8):
            rows = slice(i * 8, i * 8 + 8)
            term = share[0, rows, :] * results[0][i]
            for s in range(1, SEC):
                term = term + share[s, rows, :] * results[s][i]
            total[rows, :] += weight[k] * term
        return 0

    lax.fori_loop(0, LEV, phase_c, 0)

    for q in range(8):
        partial[q] = total[5 * q : 5 * q + 5, :]

    def reduce_copy(p):
        return pltpu.make_async_remote_copy(
            partial.at[lax.rem(me + p, 8)], others.at[p - 1],
            rs_send.at[p - 1], rs_recv.at[p - 1],
            device_id=member(lax.rem(me + p, 8)), device_id_type=MESH,
        )

    for p in range(1, 8):
        reduce_copy(p).start()

    cells_copy.wait()
    padded[...] = jnp.concatenate(
        [cells[...], jnp.full((TILES, 32), -1, jnp.int32)], axis=1
    )
    slot = lax.broadcasted_iota(jnp.int32, (128, 512), 0)

    def one_hot(t, _):
        cell = padded[pl.ds(t, 1), :]
        high[t] = jnp.where(slot == (cell >> 7), 1.0, 0.0).astype(jnp.bfloat16)
        low[t] = jnp.where(slot == (cell & 127), 1.0, 0.0).astype(jnp.bfloat16)
        return 0

    lax.fori_loop(0, TILES, one_hot, 0)

    summed = partial[me]
    for p in range(1, 8):
        reduce_copy(p).wait_recv()
        summed = summed + others[p - 1]
    for r in range(4):
        pair = jnp.concatenate([summed[r : r + 1], summed[r + 1 : r + 2]], axis=1)
        if r:
            pair = pltpu.roll(pair, 768 - 96 * r, 1)
        outgoing[r] = pair[:, :512]

    def send_copy(i):
        return pltpu.make_async_remote_copy(
            outgoing.at[i // 8], arrived.at[tile], send_sem.at[i], recv_sem.at[tile],
            device_id={
                "tile": me * 4 + i // 8, "lev": lax.rem(i, 8) // 2, "sec": lax.rem(i, 2),
            },
            device_id_type=MESH,
        )

    def is_self(i):
        return jnp.logical_and(me * 4 + i // 8 == tile, lax.rem(i, 8) == me)

    def send(i, _):
        @pl.when(jnp.logical_not(is_self(i)))
        def _():
            send_copy(i).start()

        @pl.when(is_self(i))
        def _():
            pltpu.make_async_copy(
                outgoing.at[i // 8], arrived.at[tile], recv_sem.at[tile]
            ).start()
        return 0

    hear(4)
    lax.fori_loop(0, TILES, send, 0)

    def step_of(a):
        return a + a // 2 - 2 * (a // 3)

    def accumulate(group, total):
        sources = []
        for j in range(4):
            z = lax.rem(along_z + step_of(group // 2), 4)
            x = lax.rem(along_x + step_of(2 * lax.rem(group, 2) + j // 2), 4)
            sources.append((z * 4 + x) * 2 + lax.rem(core + j % 2, 2))
        for t in sources:
            pltpu.make_async_copy(arrived.at[t], arrived.at[t], recv_sem.at[t]).wait()
        for t in sources:
            value = arrived[t]
            for _ in range(3):
                piece = value.astype(jnp.bfloat16)
                value = value - piece.astype(jnp.float32)
                spread = high[t] * jnp.broadcast_to(piece, (128, 512))
                total = total + lax.dot_general(
                    spread, low[t], (((1,), (1,)), ((), ())),
                    preferred_element_type=jnp.float32,
                )
        return total

    sums = lax.fori_loop(0, TILES // 4, accumulate, jnp.zeros((128, 128), jnp.float32))
    flux[...] = sums[: OWNED // 128]

    def finish_edges(k, _):
        for copy in edge_copies(k, 1, *edges1) + edge_copies(k, 0, *edges0):
            copy.wait_send()
        return 0

    lax.fori_loop(0, LEV, finish_edges, 0)

    @pl.when(lev > 0)
    def _():
        copy1.wait_send()
        copy0.wait_send()

    for p in range(1, 8):
        reduce_copy(p).wait_send()

    def finish(i, _):
        @pl.when(jnp.logical_not(is_self(i)))
        def _():
            send_copy(i).wait_send()
        return 0

    lax.fori_loop(0, TILES, finish, 0)


def store_kernel(adjoint, flux, adjoint_out, flux_out, sem):
    copies = (
        pltpu.make_async_copy(adjoint, adjoint_out, sem.at[0]),
        pltpu.make_async_copy(flux, flux_out, sem.at[1]),
    )
    for copy in copies:
        copy.start()
    for copy in copies:
        copy.wait()


def shards(
    forcing, courant_x, courant_y, mass_flux, limiter_code, seam_code, level_weight,
    sector_share, flux_cell,
):
    f32, bf16, i32 = jnp.float32, jnp.bfloat16, jnp.int32
    shape = jax.ShapeDtypeStruct
    dma = pltpu.SemaphoreType.DMA
    edge = pltpu.VMEM((LEV, SEC, COLS), f32)
    plane = pltpu.VMEM((SEC, ROWS, COLS), f32)
    levels = (LEV, ROWS, COLS)
    passed = pl.pallas_call(
        adjoint_kernel,
        out_shape=(
            shape(forcing.shape, f32),
            shape((OWNED // 128, 128), f32),
        ),
        in_specs=[HBM] * 9,
        out_specs=[VMEM] * 2,
        scratch_shapes=[pltpu.SMEM((2, TILES), i32), pltpu.SMEM((LEV,), f32)]
        + [pltpu.VMEM(forcing.shape, f32)] * 2
        + [pltpu.VMEM(levels, bf16)] * 3
        + [pltpu.VMEM(levels, i32)]
        + [plane]
        + [pltpu.VMEM((TILES, 480), i32), pltpu.VMEM((TILES, 512), i32)]
        + [plane] * 2
        + [edge] * 8
        + [
            pltpu.VMEM((ROWS, COLS), f32),
            pltpu.VMEM((8, 5, COLS), f32),
            pltpu.VMEM((7, 5, COLS), f32),
            pltpu.VMEM((4, 1, 512), f32),
            pltpu.VMEM((TILES, 1, 512), f32),
            pltpu.VMEM((TILES, 128, 512), bf16),
            pltpu.VMEM((TILES, 128, 512), bf16),
        ]
        + [dma((5, LEV)), dma((4,)), dma((2,)), dma((2,)), dma((2, 2, LEV)), dma((2, 2, LEV))]
        + [dma((7,)), dma((7,)), dma((TILES,)), dma((TILES,))]
        + [pltpu.SemaphoreType.REGULAR((5,))],
        compiler_params=pltpu.CompilerParams(
            collective_id=0, has_side_effects=True, vmem_limit_bytes=LIMIT_FIRST * MIB
        ),
        name="adjoint",
    )(
        *(
            pltpu.with_memory_space_constraint(x, pltpu.HBM)
            for x in (
                seam_code.T, level_weight, forcing, courant_x, courant_y, mass_flux,
                limiter_code, sector_share, flux_cell,
            )
        ),
    )
    adjoint, flux = pl.pallas_call(
        store_kernel,
        out_shape=(shape(forcing.shape, f32), shape((OWNED // 128, 128), f32)),
        in_specs=[VMEM] * 2,
        out_specs=[HBM] * 2,
        scratch_shapes=[dma((2,))],
        compiler_params=pltpu.CompilerParams(vmem_limit_bytes=LIMIT_SECOND * MIB),
        name="store",
    )(*passed)
    return adjoint, flux.reshape(-1)


def solution(mesh):
    placed = (
        P("sec", "lev", "tile", None),
        P("lev", "tile", None),
        P("lev", "tile", None),
        P("lev", "tile", None),
        P("lev", "tile", None),
        P(),
        P("lev"),
        P("sec", "tile", None),
        P("tile", None),
    )
    return jax.shard_map(
        shards,
        mesh=mesh,
        in_specs=placed,
        out_specs=(P("sec", "lev", "tile", None), P("tile")),
        check_vma=False,
    )
```

```python
import functools

import jax
import jax.numpy as jnp
from jax import lax
from jax.experimental import pallas as pl
from jax.experimental.pallas import tpu as pltpu
from jax.sharding import PartitionSpec as P

SEC, LEV, ROWS, COLS = 4, 18, 40, 384
TILES = 32
OWNED = 15360
MESH = pl.DeviceIdType.MESH
HBM = pl.BlockSpec(memory_space=pltpu.HBM)
VMEM = pl.BlockSpec(memory_space=pltpu.VMEM)
SMEM = pl.BlockSpec(memory_space=pltpu.SMEM)
MIB = 1024 * 1024
LIMIT_FIRST = 40
LIMIT_SECOND = 8
CHUNKS = ((0, 16), (16, 16), (32, 8))
PARTS = ((0, 8), (32, 8), (8, 24))
EDGE1_AT, EDGE0_AT, REST0_AT = 0, 0, 2


def coefficients(courant, code, bit):
    size = jnp.abs(courant)
    rest = 1.0 - size
    twice = jnp.where((code & (1 << bit)) != 0, size * rest, 0.0)
    spread = 0.5 * twice
    positive = jnp.maximum(courant, 0.0)
    ahead = positive - spread
    back = (size - positive) - spread
    return ahead, back


def second_coefficients(courant, code, bit):
    ahead, back = coefficients(courant, code, bit)
    lane = lax.broadcasted_iota(jnp.int32, ahead.shape, 1)
    ahead = jnp.where(lane == COLS - 1, 0.0, ahead)
    back = jnp.where(lane == 0, 0.0, back)
    return ahead, back, 1.0 - ahead - back


def rims(left, right, flag_left, flag_right):
    both = jnp.concatenate([left, right], axis=0)
    lane = lax.broadcasted_iota(jnp.int32, (2 * SEC, 128), 1)
    parts = [
        jnp.take_along_axis(both[:, i * 128 : (i + 1) * 128], 127 - lane, axis=1)
        for i in (2, 1, 0)
    ]
    row = lax.broadcasted_iota(jnp.int32, both.shape, 0)
    flag = jnp.where(row < SEC, flag_left, flag_right)
    return jnp.where(flag == 1, jnp.concatenate(parts, axis=1), both)


def first_sweep(blocks, edges, sector, coefs):
    sub = lax.broadcasted_iota(jnp.int32, (8, COLS), 0)
    low = jnp.broadcast_to(edges[sector : sector + 1], (8, COLS))
    high = jnp.broadcast_to(edges[SEC + sector : SEC + sector + 1], (8, COLS))
    down = [low] + [pltpu.roll(b, 1, 0) for b in blocks]
    up = [pltpu.roll(b, 7, 0) for b in blocks] + [high]
    out = []
    for i, block in enumerate(blocks):
        ahead, back, centre = coefs[i]
        previous = jnp.where(sub == 0, down[i], down[i + 1])
        following = jnp.where(sub == 7, up[i + 1], up[i])
        out.append(centre * block + ahead * following + back * previous)
    return out


def first_coefficients(courant, code, bit):
    ahead, back = coefficients(courant.astype(jnp.float32), code, bit)
    centre = 1.0 - ahead - back
    return [
        (ahead[i : i + 8], back[i : i + 8], centre[i : i + 8]) for i in range(0, ROWS, 8)
    ]


def adjoint_kernel(
    seam_code,
    level_weight,
    forcing,
    courant_x,
    courant_y,
    mass_flux,
    limiter,
    sector_share,
    flux_cell,
    out,
    flux,
    seam,
    weight,
    field,
    swept,
    cx,
    cy,
    mf,
    code,
    share,
    cells,
    padded,
    halo1,
    halo0,
    first1,
    last1,
    left1,
    right1,
    first0,
    last0,
    left0,
    right0,
    total,
    partial,
    others,
    outgoing,
    arrived,
    high,
    low,
    load_sem,
    extra_sem,
    lev_send,
    lev_recv,
    edge_send,
    edge_recv,
    rs_send,
    rs_recv,
    send_sem,
    recv_sem,
    ready,
):
    tile, lev, sec = lax.axis_index("tile"), lax.axis_index("lev"), lax.axis_index("sec")
    after, before = lax.rem(tile + 1, TILES), lax.rem(tile + TILES - 1, TILES)
    lower = lax.rem(lev + 3, 4)
    me = lev * 2 + sec

    def member(q):
        return {"tile": tile, "lev": q // 2, "sec": lax.rem(q, 2)}

    def loads(i):
        pair = pl.ds(2 * i, 2)
        return (
            pltpu.make_async_copy(forcing.at[:, pair], field.at[:, pair], load_sem.at[0, i]),
            pltpu.make_async_copy(mass_flux.at[pair], mf.at[pair], load_sem.at[1, i]),
            pltpu.make_async_copy(courant_y.at[pair], cy.at[pair], load_sem.at[2, i]),
            pltpu.make_async_copy(limiter.at[pair], code.at[pair], load_sem.at[3, i]),
            pltpu.make_async_copy(courant_x.at[pair], cx.at[pair], load_sem.at[4, i]),
        )

    def start_loads(i, _):
        for copy in loads(i)[:4]:
            copy.start()
        return 0

    def start_late_loads(i, _):
        loads(i)[4].start()
        return 0

    share_copy = pltpu.make_async_copy(sector_share, share, extra_sem.at[0])
    cells_copy = pltpu.make_async_copy(flux_cell, cells, extra_sem.at[1])
    seam_copy = pltpu.make_async_copy(seam_code, seam, extra_sem.at[2])
    weight_copy = pltpu.make_async_copy(level_weight, weight, extra_sem.at[3])

    barrier = pltpu.get_barrier_semaphore()
    along_z, along_x, core = tile // 8, lax.rem(tile // 2, 4), lax.rem(tile, 2)

    def tile_at(z, x, c):
        return {"tile": (lax.rem(z, 4) * 4 + lax.rem(x, 4)) * 2 + lax.rem(c, 2)}

    beside_z = [tile_at(along_z + i, along_x, core) for i in (1, 3)]
    beside_x = [tile_at(along_z, along_x + i, core) for i in (1, 3)]
    near = [{"tile": after}, {"tile": before}] + beside_z + beside_x
    near += [member(lax.rem(me + p, 8)) for p in range(1, 8)]
    for device in near:
        pl.semaphore_signal(barrier, inc=1, device_id=device, device_id_type=MESH)

    stages = (beside_z, beside_z, beside_x, beside_x, [tile_at(along_z, along_x, core + 1)])

    def tell(i):
        for device in stages[i]:
            pl.semaphore_signal(ready.at[i], inc=1, device_id=device, device_id_type=MESH)

    def hear(i):
        pl.semaphore_wait(ready.at[i], len(stages[i]))

    lax.fori_loop(0, LEV // 2, start_loads, 0)
    lax.fori_loop(0, LEV // 2, start_late_loads, 0)
    for copy in (share_copy, cells_copy, seam_copy, weight_copy):
        copy.start()

    def level_copies(source, halo, step):
        return [
            pltpu.make_async_remote_copy(
                source.at[:, 0, pl.ds(start, size)], halo.at[:, pl.ds(start, size)],
                lev_send.at[step, i], lev_recv.at[step, i],
                device_id={"lev": lower}, device_id_type=MESH,
            )
            for i, (start, size) in enumerate(PARTS)
        ]

    def edge_copies(group, step, first, last, left, right):
        if isinstance(group, int) and group >= 4:
            part = pl.ds(12 + group, 1)
        else:
            part = pl.ds(4 * group, 4)
        return (
            pltpu.make_async_remote_copy(
                first.at[part], right.at[part],
                edge_send.at[step, 0, group], edge_recv.at[step, 0, group],
                device_id={"tile": before}, device_id_type=MESH,
            ),
            pltpu.make_async_remote_copy(
                last.at[part], left.at[part],
                edge_send.at[step, 1, group], edge_recv.at[step, 1, group],
                device_id={"tile": after}, device_id_type=MESH,
            ),
        )

    def start_levels(source, halo, step):
        @pl.when(lev > 0)
        def _():
            for copy in level_copies(source, halo, step):
                copy.start()

    def meet():
        pl.semaphore_wait(barrier, len(near))
        tell(0)

        start_levels(forcing, halo1, 1)

    def vertical_second(k, above, bit, step, first, last, left, right, chunks=CHUNKS):
        for start, size in chunks:
            rows = slice(start, start + size)
            mixing = mf[k, rows, :].astype(jnp.float32)
            ahead, back, centre = second_coefficients(
                cy[k, rows, :].astype(jnp.float32), code[k, rows, :], bit
            )
            for s in range(SEC):
                value = field[s, k, rows, :]
                value = value + mixing * (above(s, rows) - value)
                value = (
                    centre * value
                    + ahead * pltpu.roll(value, COLS - 1, 1)
                    + back * pltpu.roll(value, 1, 1)
                )
                swept[s, k, rows, :] = value
                if start == 0:
                    first[k, s : s + 1, :] = value[:1]
                if start == 32:
                    last[k, s : s + 1, :] = value[7:]

    def send_edges(group, step, edges):
        for copy in edge_copies(group, step, *edges):
            copy.start()

    def take_edges(group, step, edges):
        for copy in edge_copies(group, step, *edges):
            copy.wait_recv()

    edges1 = (first1, last1, left1, right1)
    edges0 = (first0, last0, left0, right0)
    step1 = (3, 1) + edges1
    step0 = (1, 0) + edges0

    def inner_level(k, step_args):
        vertical_second(k, lambda s, rows: field[s, k + 1, rows, :], *step_args)

    loads(0)[0].wait()

    def phase_a(g, _):
        for i in range(2):
            for copy in loads(2 * g + i)[1:4]:
                copy.wait()
            loads(2 * g + i + 1)[0].wait()
        for j in range(4):
            inner_level(4 * g + j, step1)

        @pl.when(g == 0)
        def _():
            meet()

        send_edges(g, 1, edges1)
        return 0

    lax.fori_loop(0, 4, phase_a, 0)
    for copy in loads(8)[1:4]:
        copy.wait()
    inner_level(16, step1)
    send_edges(4, 1, edges1)

    def top_level(source, halo, step, step_args, parts):
        copies = level_copies(source, halo, step)

        @pl.when(lev < 3)
        def _():
            for i in parts:
                copies[i].wait_recv()

        @pl.when(lev == 3)
        def _():
            for i in parts:
                start, size = PARTS[i]
                for s in range(SEC):
                    halo[s, start : start + size] = field[s, LEV - 1, start : start + size]

        vertical_second(
            LEV - 1, lambda s, rows: halo[s, rows, :], *step_args,
            chunks=[PARTS[i] for i in parts],
        )

    cells_copy.wait()
    padded[...] = jnp.concatenate(
        [cells[...], jnp.full((TILES, 32), -1, jnp.int32)], axis=1
    )
    slot = lax.broadcasted_iota(jnp.int32, (128, 512), 0)

    def one_hot(t, _):
        cell = padded[pl.ds(t, 1), :]
        high[t] = jnp.where(slot == (cell >> 7), 1.0, 0.0).astype(jnp.bfloat16)
        low[t] = jnp.where(slot == (cell & 127), 1.0, 0.0).astype(jnp.bfloat16)
        return 0

    lax.fori_loop(0, TILES, one_hot, 0)

    seam_copy.wait()
    flag_left, flag_right = seam[0, tile], seam[1, tile]

    def first_dimension(k, edges, bit, target):
        rim = rims(edges[2][k], edges[3][k], flag_left, flag_right)
        coefs = first_coefficients(cx[k], code[k], bit)
        results = []
        for s in range(SEC):
            blocks = [swept[s, k, i : i + 8, :] for i in range(0, ROWS, 8)]
            blocks = first_sweep(blocks, rim, s, coefs)
            for i, block in enumerate(blocks):
                target[s, k, i * 8 : i * 8 + 8, :] = block
            results.append(blocks)
        return results

    hear(0)
    tell(1)

    def first_group(g):
        take_edges(g, 1, edges1)
        for i in range(2):
            loads(2 * g + i)[4].wait()
        for j in range(4):
            first_dimension(4 * g + j, edges1, 2, field)

    def second_group(g):
        for j in range(4):
            inner_level(4 * g + j, step0)
        send_edges(g, 0, edges0)

    def early_top1():
        top_level(forcing, halo1, 1, step1, (0, 1))
        send_edges(5, 1, edges1)

    def early_top0():
        take_edges(5, 1, edges1)
        first_dimension(17, edges1, 2, field)
        inner_level(16, step0)
        send_edges(4, 0, edges0)
        top_level(field, halo0, 0, step0, (0, 1))
        send_edges(5, 0, edges0)

    first_group(0)
    start_levels(field, halo0, 0)

    def phase_b(g, _):
        first_group(g + 1)
        second_group(g)

        @pl.when(g == EDGE1_AT)
        def _():
            early_top1()

        @pl.when(g == 1)
        def _():
            hear(1)
            tell(2)

        return 0

    lax.fori_loop(0, 3, phase_b, 0)
    take_edges(4, 1, edges1)
    loads(8)[4].wait()
    first_dimension(16, edges1, 2, field)
    second_group(3)
    hear(2)
    tell(3)
    top_level(forcing, halo1, 1, step1, (2,))

    share_copy.wait()
    weight_copy.wait()
    total[...] = jnp.zeros_like(total)

    def last_level(k):
        results = first_dimension(k, edges0, 0, out)
        for i in range(ROWS // 8):
            rows = slice(i * 8, i * 8 + 8)
            term = share[0, rows, :] * results[0][i]
            for s in range(1, SEC):
                term = term + share[s, rows, :] * results[s][i]
            total[rows, :] += weight[k] * term

    def phase_c(g, _):
        @pl.when(g == EDGE0_AT)
        def _():
            early_top0()

        @pl.when(g == REST0_AT)
        def _():
            top_level(field, halo0, 0, step0, (2,))

        @pl.when(g == 1)
        def _():
            hear(3)
            tell(4)

        take_edges(g, 0, edges0)
        for j in range(4):
            last_level(4 * g + j)
        return 0

    lax.fori_loop(0, 4, phase_c, 0)
    take_edges(4, 0, edges0)
    last_level(16)
    take_edges(5, 0, edges0)
    last_level(17)

    for q in range(8):
        partial[q] = total[5 * q : 5 * q + 5, :]

    def reduce_copy(p):
        return pltpu.make_async_remote_copy(
            partial.at[lax.rem(me + p, 8)], others.at[p - 1],
            rs_send.at[p - 1], rs_recv.at[p - 1],
            device_id=member(lax.rem(me + p, 8)), device_id_type=MESH,
        )

    for p in range(1, 8):
        reduce_copy(p).start()

    summed = partial[me]
    for p in range(1, 8):
        reduce_copy(p).wait_recv()
        summed = summed + others[p - 1]
    for r in range(4):
        pair = jnp.concatenate([summed[r : r + 1], summed[r + 1 : r + 2]], axis=1)
        if r:
            pair = pltpu.roll(pair, 768 - 96 * r, 1)
        outgoing[r] = pair[:, :512]

    def send_copy(i):
        return pltpu.make_async_remote_copy(
            outgoing.at[i // 8], arrived.at[tile], send_sem.at[i], recv_sem.at[tile],
            device_id={
                "tile": me * 4 + i // 8, "lev": lax.rem(i, 8) // 2, "sec": lax.rem(i, 2),
            },
            device_id_type=MESH,
        )

    def is_self(i):
        return jnp.logical_and(me * 4 + i // 8 == tile, lax.rem(i, 8) == me)

    def send(i, _):
        @pl.when(jnp.logical_not(is_self(i)))
        def _():
            send_copy(i).start()

        @pl.when(is_self(i))
        def _():
            pltpu.make_async_copy(
                outgoing.at[i // 8], arrived.at[tile], recv_sem.at[tile]
            ).start()
        return 0

    hear(4)
    lax.fori_loop(0, TILES, send, 0)

    def step_of(a):
        return a + a // 2 - 2 * (a // 3)

    def accumulate(group, total):
        sources = []
        for j in range(4):
            z = lax.rem(along_z + step_of(group // 2), 4)
            x = lax.rem(along_x + step_of(2 * lax.rem(group, 2) + j // 2), 4)
            sources.append((z * 4 + x) * 2 + lax.rem(core + j % 2, 2))
        for t in sources:
            pltpu.make_async_copy(arrived.at[t], arrived.at[t], recv_sem.at[t]).wait()
        for t in sources:
            value = arrived[t]
            for _ in range(2):
                piece = value.astype(jnp.bfloat16)
                value = value - piece.astype(jnp.float32)
                spread = high[t] * jnp.broadcast_to(piece, (128, 512))
                total = total + lax.dot_general(
                    spread, low[t], (((1,), (1,)), ((), ())),
                    preferred_element_type=jnp.float32,
                )
        return total

    sums = lax.fori_loop(0, TILES // 4, accumulate, jnp.zeros((128, 128), jnp.float32))
    flux[...] = sums[: OWNED // 128]

    for group in range(6):
        for copy in edge_copies(group, 1, *edges1) + edge_copies(group, 0, *edges0):
            copy.wait_send()

    @pl.when(lev > 0)
    def _():
        for copy in level_copies(forcing, halo1, 1) + level_copies(field, halo0, 0):
            copy.wait_send()

    for p in range(1, 8):
        reduce_copy(p).wait_send()

    def finish(i, _):
        @pl.when(jnp.logical_not(is_self(i)))
        def _():
            send_copy(i).wait_send()
        return 0

    lax.fori_loop(0, TILES, finish, 0)


def store_kernel(adjoint, flux, adjoint_out, flux_out, sem):
    copies = (
        pltpu.make_async_copy(adjoint, adjoint_out, sem.at[0]),
        pltpu.make_async_copy(flux, flux_out, sem.at[1]),
    )
    for copy in copies:
        copy.start()
    for copy in copies:
        copy.wait()


def shards(
    forcing, courant_x, courant_y, mass_flux, limiter_code, seam_code, level_weight,
    sector_share, flux_cell,
):
    f32, bf16, i32 = jnp.float32, jnp.bfloat16, jnp.int32
    shape = jax.ShapeDtypeStruct
    dma = pltpu.SemaphoreType.DMA
    edge = pltpu.VMEM((LEV, SEC, COLS), f32)
    plane = pltpu.VMEM((SEC, ROWS, COLS), f32)
    levels = (LEV, ROWS, COLS)
    passed = pl.pallas_call(
        adjoint_kernel,
        out_shape=(
            shape(forcing.shape, f32),
            shape((OWNED // 128, 128), f32),
        ),
        in_specs=[HBM] * 9,
        out_specs=[VMEM] * 2,
        scratch_shapes=[pltpu.SMEM((2, TILES), i32), pltpu.SMEM((LEV,), f32)]
        + [pltpu.VMEM(forcing.shape, f32)] * 2
        + [pltpu.VMEM(levels, bf16)] * 3
        + [pltpu.VMEM(levels, i32)]
        + [plane]
        + [pltpu.VMEM((TILES, 480), i32), pltpu.VMEM((TILES, 512), i32)]
        + [plane] * 2
        + [edge] * 8
        + [
            pltpu.VMEM((ROWS, COLS), f32),
            pltpu.VMEM((8, 5, COLS), f32),
            pltpu.VMEM((7, 5, COLS), f32),
            pltpu.VMEM((4, 1, 512), f32),
            pltpu.VMEM((TILES, 1, 512), f32),
            pltpu.VMEM((TILES, 128, 512), bf16),
            pltpu.VMEM((TILES, 128, 512), bf16),
        ]
        + [dma((5, LEV // 2)), dma((4,)), dma((2, 3)), dma((2, 3)), dma((2, 2, 6)), dma((2, 2, 6))]
        + [dma((7,)), dma((7,)), dma((TILES,)), dma((TILES,))]
        + [pltpu.SemaphoreType.REGULAR((5,))],
        compiler_params=pltpu.CompilerParams(
            collective_id=0, has_side_effects=True, vmem_limit_bytes=LIMIT_FIRST * MIB
        ),
        name="adjoint",
    )(
        *(
            pltpu.with_memory_space_constraint(x, pltpu.HBM)
            for x in (
                seam_code.T, level_weight, forcing, courant_x, courant_y, mass_flux,
                limiter_code, sector_share, flux_cell,
            )
        ),
    )
    adjoint, flux = pl.pallas_call(
        store_kernel,
        out_shape=(shape(forcing.shape, f32), shape((OWNED // 128, 128), f32)),
        in_specs=[VMEM] * 2,
        out_specs=[HBM] * 2,
        scratch_shapes=[dma((2,))],
        compiler_params=pltpu.CompilerParams(vmem_limit_bytes=LIMIT_SECOND * MIB),
        name="store",
    )(*passed)
    return adjoint, flux.reshape(-1)


def solution(mesh):
    placed = (
        P("sec", "lev", "tile", None),
        P("lev", "tile", None),
        P("lev", "tile", None),
        P("lev", "tile", None),
        P("lev", "tile", None),
        P(),
        P("lev"),
        P("sec", "tile", None),
        P("tile", None),
    )
    return jax.shard_map(
        shards,
        mesh=mesh,
        in_specs=placed,
        out_specs=(P("sec", "lev", "tile", None), P("tile")),
        check_vma=False,
    )
```

```python
import functools

import jax
import jax.numpy as jnp
from jax import lax
from jax.experimental import pallas as pl
from jax.experimental.pallas import tpu as pltpu
from jax.sharding import PartitionSpec as P

SEC, LEV, ROWS, COLS = 4, 18, 40, 384
TILES = 32
OWNED = 15360
MESH = pl.DeviceIdType.MESH
HBM = pl.BlockSpec(memory_space=pltpu.HBM)
VMEM = pl.BlockSpec(memory_space=pltpu.VMEM)
SMEM = pl.BlockSpec(memory_space=pltpu.SMEM)
MIB = 1024 * 1024
LIMIT_FIRST = 40
LIMIT_SECOND = 8
CHUNKS = ((0, 16), (16, 16), (32, 8))
REST0_AT = 1


def coefficients(courant, code, bit):
    size = jnp.abs(courant)
    rest = 1.0 - size
    twice = jnp.where((code & (1 << bit)) != 0, size * rest, 0.0)
    spread = 0.5 * twice
    positive = jnp.maximum(courant, 0.0)
    ahead = positive - spread
    back = (size - positive) - spread
    return ahead, back


def second_coefficients(courant, code, bit):
    ahead, back = coefficients(courant, code, bit)
    lane = lax.broadcasted_iota(jnp.int32, ahead.shape, 1)
    ahead = jnp.where(lane == COLS - 1, 0.0, ahead)
    back = jnp.where(lane == 0, 0.0, back)
    return ahead, back, 1.0 - ahead - back


def rims(left, right, flag_left, flag_right):
    both = jnp.concatenate([left, right], axis=0)
    lane = lax.broadcasted_iota(jnp.int32, (2 * SEC, 128), 1)
    parts = [
        jnp.take_along_axis(both[:, i * 128 : (i + 1) * 128], 127 - lane, axis=1)
        for i in (2, 1, 0)
    ]
    row = lax.broadcasted_iota(jnp.int32, both.shape, 0)
    flag = jnp.where(row < SEC, flag_left, flag_right)
    return jnp.where(flag == 1, jnp.concatenate(parts, axis=1), both)


def first_sweep(blocks, edges, sector, coefs):
    sub = lax.broadcasted_iota(jnp.int32, (8, COLS), 0)
    low = jnp.broadcast_to(edges[sector : sector + 1], (8, COLS))
    high = jnp.broadcast_to(edges[SEC + sector : SEC + sector + 1], (8, COLS))
    down = [low] + [pltpu.roll(b, 1, 0) for b in blocks]
    up = [pltpu.roll(b, 7, 0) for b in blocks] + [high]
    out = []
    for i, block in enumerate(blocks):
        ahead, back, centre = coefs[i]
        previous = jnp.where(sub == 0, down[i], down[i + 1])
        following = jnp.where(sub == 7, up[i + 1], up[i])
        out.append(centre * block + ahead * following + back * previous)
    return out


def first_coefficients(courant, code, bit):
    ahead, back = coefficients(courant.astype(jnp.float32), code, bit)
    centre = 1.0 - ahead - back
    return [
        (ahead[i : i + 8], back[i : i + 8], centre[i : i + 8]) for i in range(0, ROWS, 8)
    ]


def adjoint_kernel(
    seam_code,
    level_weight,
    forcing,
    courant_x,
    courant_y,
    mass_flux,
    limiter,
    sector_share,
    flux_cell,
    out,
    flux,
    seam,
    weight,
    field,
    swept,
    cx,
    cy,
    mf,
    code,
    share,
    cells,
    padded,
    halo1,
    halo0,
    rows_out,
    rows_in,
    first1,
    last1,
    left1,
    right1,
    first0,
    last0,
    left0,
    right0,
    total,
    partial,
    others,
    outgoing,
    arrived,
    high,
    low,
    load_sem,
    extra_sem,
    lev_send,
    lev_recv,
    edge_send,
    edge_recv,
    rs_send,
    rs_recv,
    send_sem,
    recv_sem,
    ready,
):
    tile, lev, sec = lax.axis_index("tile"), lax.axis_index("lev"), lax.axis_index("sec")
    after, before = lax.rem(tile + 1, TILES), lax.rem(tile + TILES - 1, TILES)
    lower = lax.rem(lev + 3, 4)
    me = lev * 2 + sec

    def member(q):
        return {"tile": tile, "lev": q // 2, "sec": lax.rem(q, 2)}

    def loads(i):
        pair = pl.ds(2 * i, 2)
        return (
            pltpu.make_async_copy(forcing.at[:, pair], field.at[:, pair], load_sem.at[0, i]),
            pltpu.make_async_copy(mass_flux.at[pair], mf.at[pair], load_sem.at[1, i]),
            pltpu.make_async_copy(courant_y.at[pair], cy.at[pair], load_sem.at[2, i]),
            pltpu.make_async_copy(limiter.at[pair], code.at[pair], load_sem.at[3, i]),
            pltpu.make_async_copy(courant_x.at[pair], cx.at[pair], load_sem.at[4, i]),
        )

    def start_loads(i, _):
        for copy in loads(i)[:4]:
            copy.start()
        return 0

    def start_late_loads(i, _):
        loads(i)[4].start()
        return 0

    share_copy = pltpu.make_async_copy(sector_share, share, extra_sem.at[0])
    cells_copy = pltpu.make_async_copy(flux_cell, cells, extra_sem.at[1])
    seam_copy = pltpu.make_async_copy(seam_code, seam, extra_sem.at[2])
    weight_copy = pltpu.make_async_copy(level_weight, weight, extra_sem.at[3])

    barrier = pltpu.get_barrier_semaphore()
    along_z, along_x, core = tile // 8, lax.rem(tile // 2, 4), lax.rem(tile, 2)

    def tile_at(z, x, c):
        return {"tile": (lax.rem(z, 4) * 4 + lax.rem(x, 4)) * 2 + lax.rem(c, 2)}

    beside_z = [tile_at(along_z + i, along_x, core) for i in (1, 3)]
    beside_x = [tile_at(along_z, along_x + i, core) for i in (1, 3)]
    near = [{"tile": after}, {"tile": before}] + beside_z + beside_x
    near += [member(lax.rem(me + p, 8)) for p in range(1, 8)]
    for device in near:
        pl.semaphore_signal(barrier, inc=1, device_id=device, device_id_type=MESH)

    stages = (beside_z, beside_z, beside_x, beside_x, [tile_at(along_z, along_x, core + 1)])

    def tell(i):
        for device in stages[i]:
            pl.semaphore_signal(ready.at[i], inc=1, device_id=device, device_id_type=MESH)

    def hear(i):
        pl.semaphore_wait(ready.at[i], len(stages[i]))

    lax.fori_loop(0, LEV // 2, start_loads, 0)
    lax.fori_loop(0, LEV // 2, start_late_loads, 0)
    for copy in (share_copy, cells_copy, seam_copy, weight_copy):
        copy.start()

    def level_copies(source, halo, step):
        return (
            pltpu.make_async_remote_copy(
                rows_out.at[step], rows_in.at[step],
                lev_send.at[step, 0], lev_recv.at[step, 0],
                device_id={"lev": lower}, device_id_type=MESH,
            ),
            pltpu.make_async_remote_copy(
                source.at[:, 0], halo, lev_send.at[step, 1], lev_recv.at[step, 1],
                device_id={"lev": lower}, device_id_type=MESH,
            ),
        )

    def edge_copies(group, step, first, last, left, right):
        if isinstance(group, int) and group >= 4:
            part = pl.ds(12 + group, 1)
        else:
            part = pl.ds(4 * group, 4)
        return (
            pltpu.make_async_remote_copy(
                first.at[part], right.at[part],
                edge_send.at[step, 0, group], edge_recv.at[step, 0, group],
                device_id={"tile": before}, device_id_type=MESH,
            ),
            pltpu.make_async_remote_copy(
                last.at[part], left.at[part],
                edge_send.at[step, 1, group], edge_recv.at[step, 1, group],
                device_id={"tile": after}, device_id_type=MESH,
            ),
        )

    def start_levels(source, halo, step):
        for i, row in enumerate((0, ROWS - 1)):
            for s in range(SEC):
                rows_out[step, i, s : s + 1, :] = field[s, 0, row : row + 1, :]

        @pl.when(lev > 0)
        def _():
            for copy in level_copies(source, halo, step):
                copy.start()

    def meet():
        pl.semaphore_wait(barrier, len(near))
        tell(0)

        start_levels(forcing, halo1, 1)

    def vertical_second(k, above, bit, step, first, last, left, right, rims_too=True):
        for start, size in CHUNKS:
            rows = slice(start, start + size)
            mixing = mf[k, rows, :].astype(jnp.float32)
            ahead, back, centre = second_coefficients(
                cy[k, rows, :].astype(jnp.float32), code[k, rows, :], bit
            )
            for s in range(SEC):
                value = field[s, k, rows, :]
                value = value + mixing * (above(s, rows) - value)
                value = (
                    centre * value
                    + ahead * pltpu.roll(value, COLS - 1, 1)
                    + back * pltpu.roll(value, 1, 1)
                )
                swept[s, k, rows, :] = value
                if rims_too and start == 0:
                    first[k, s : s + 1, :] = value[:1]
                if rims_too and start == 32:
                    last[k, s : s + 1, :] = value[7:]

    def send_edges(group, step, edges):
        for copy in edge_copies(group, step, *edges):
            copy.start()

    def take_edges(group, step, edges):
        for copy in edge_copies(group, step, *edges):
            copy.wait_recv()

    edges1 = (first1, last1, left1, right1)
    edges0 = (first0, last0, left0, right0)
    step1 = (3, 1) + edges1
    step0 = (1, 0) + edges0

    def inner_level(k, step_args):
        vertical_second(k, lambda s, rows: field[s, k + 1, rows, :], *step_args)

    loads(0)[0].wait()

    def phase_a(g, _):
        for i in range(2):
            for copy in loads(2 * g + i)[1:4]:
                copy.wait()
            loads(2 * g + i + 1)[0].wait()
        for j in range(4):
            inner_level(4 * g + j, step1)

        @pl.when(g == 0)
        def _():
            meet()

        send_edges(g, 1, edges1)
        return 0

    lax.fori_loop(0, 4, phase_a, 0)
    for copy in loads(8)[1:4]:
        copy.wait()
    inner_level(16, step1)
    send_edges(4, 1, edges1)

    def top_level(source, halo, step, step_args):
        @pl.when(lev < 3)
        def _():
            level_copies(source, halo, step)[1].wait_recv()

        @pl.when(lev == 3)
        def _():
            for s in range(SEC):
                halo[s] = field[s, LEV - 1]

        vertical_second(
            LEV - 1, lambda s, rows: halo[s, rows, :], *step_args, rims_too=False
        )

    def top_rims(source, halo, step, bit, targets):
        @pl.when(lev < 3)
        def _():
            level_copies(source, halo, step)[0].wait_recv()

        for i, (start, at, target) in enumerate(((0, 0, targets[0]), (32, 7, targets[1]))):
            rows = slice(start, start + 8)
            value = jnp.concatenate(
                [field[s, LEV - 1, start + at : start + at + 1, :] for s in range(SEC)], axis=0
            )
            ahead, back, centre = second_coefficients(
                cy[LEV - 1, rows, :].astype(jnp.float32), code[LEV - 1, rows, :], bit
            )
            mixing = mf[LEV - 1, rows, :].astype(jnp.float32)
            ahead, back, centre, mixing = [
                x[at : at + 1] for x in (ahead, back, centre, mixing)
            ]
            above = jnp.where(lev == 3, value, rows_in[step, i])
            value = value + mixing * (above - value)
            target[LEV - 1] = (
                centre * value
                + ahead * pltpu.roll(value, COLS - 1, 1)
                + back * pltpu.roll(value, 1, 1)
            )
        send_edges(5, step, edges1 if step else edges0)

    cells_copy.wait()
    padded[...] = jnp.concatenate(
        [cells[...], jnp.full((TILES, 32), -1, jnp.int32)], axis=1
    )
    slot = lax.broadcasted_iota(jnp.int32, (128, 512), 0)

    def one_hot(t, _):
        cell = padded[pl.ds(t, 1), :]
        high[t] = jnp.where(slot == (cell >> 7), 1.0, 0.0).astype(jnp.bfloat16)
        low[t] = jnp.where(slot == (cell & 127), 1.0, 0.0).astype(jnp.bfloat16)
        return 0

    lax.fori_loop(0, TILES, one_hot, 0)

    seam_copy.wait()
    flag_left, flag_right = seam[0, tile], seam[1, tile]

    def first_dimension(k, edges, bit, target):
        rim = rims(edges[2][k], edges[3][k], flag_left, flag_right)
        coefs = first_coefficients(cx[k], code[k], bit)
        results = []
        for s in range(SEC):
            blocks = [swept[s, k, i : i + 8, :] for i in range(0, ROWS, 8)]
            blocks = first_sweep(blocks, rim, s, coefs)
            for i, block in enumerate(blocks):
                target[s, k, i * 8 : i * 8 + 8, :] = block
            results.append(blocks)
        return results

    hear(0)
    tell(1)

    def first_group(g, least=0):
        if least == 0:
            take_edges(g, 1, edges1)
            for i in range(2):
                loads(2 * g + i)[4].wait()
        for j in range(least, 4):
            first_dimension(4 * g + j, edges1, 2, field)

    def second_group(g):
        for j in range(4):
            inner_level(4 * g + j, step0)
        send_edges(g, 0, edges0)

    top_rims(forcing, halo1, 1, 3, (first1, last1))
    take_edges(0, 1, edges1)
    for i in range(2):
        loads(i)[4].wait()
    first_dimension(0, edges1, 2, field)
    start_levels(field, halo0, 0)
    first_group(0, 1)

    def phase_b(g, _):
        first_group(g + 1)
        second_group(g)

        @pl.when(g == 1)
        def _():
            hear(1)
            tell(2)

        return 0

    lax.fori_loop(0, 3, phase_b, 0)
    take_edges(4, 1, edges1)
    loads(8)[4].wait()
    first_dimension(16, edges1, 2, field)
    second_group(3)
    hear(2)
    tell(3)
    top_level(forcing, halo1, 1, step1)
    take_edges(5, 1, edges1)
    first_dimension(17, edges1, 2, field)
    top_rims(field, halo0, 0, 1, (first0, last0))
    inner_level(16, step0)
    send_edges(4, 0, edges0)

    share_copy.wait()
    weight_copy.wait()
    total[...] = jnp.zeros_like(total)

    def last_level(k):
        results = first_dimension(k, edges0, 0, out)
        for i in range(ROWS // 8):
            rows = slice(i * 8, i * 8 + 8)
            term = share[0, rows, :] * results[0][i]
            for s in range(1, SEC):
                term = term + share[s, rows, :] * results[s][i]
            total[rows, :] += weight[k] * term

    def phase_c(g, _):
        @pl.when(g == REST0_AT)
        def _():
            top_level(field, halo0, 0, step0)

        @pl.when(g == 1)
        def _():
            hear(3)
            tell(4)

        take_edges(g, 0, edges0)
        for j in range(4):
            last_level(4 * g + j)
        return 0

    lax.fori_loop(0, 4, phase_c, 0)
    take_edges(4, 0, edges0)
    last_level(16)
    take_edges(5, 0, edges0)
    last_level(17)

    for q in range(8):
        partial[q] = total[5 * q : 5 * q + 5, :]

    def reduce_copy(p):
        return pltpu.make_async_remote_copy(
            partial.at[lax.rem(me + p, 8)], others.at[p - 1],
            rs_send.at[p - 1], rs_recv.at[p - 1],
            device_id=member(lax.rem(me + p, 8)), device_id_type=MESH,
        )

    for p in range(1, 8):
        reduce_copy(p).start()

    summed = partial[me]
    for p in range(1, 8):
        reduce_copy(p).wait_recv()
        summed = summed + others[p - 1]
    for r in range(4):
        pair = jnp.concatenate([summed[r : r + 1], summed[r + 1 : r + 2]], axis=1)
        if r:
            pair = pltpu.roll(pair, 768 - 96 * r, 1)
        outgoing[r] = pair[:, :512]

    def send_copy(i):
        return pltpu.make_async_remote_copy(
            outgoing.at[i // 8], arrived.at[tile], send_sem.at[i], recv_sem.at[tile],
            device_id={
                "tile": me * 4 + i // 8, "lev": lax.rem(i, 8) // 2, "sec": lax.rem(i, 2),
            },
            device_id_type=MESH,
        )

    def is_self(i):
        return jnp.logical_and(me * 4 + i // 8 == tile, lax.rem(i, 8) == me)

    def send(i, _):
        @pl.when(jnp.logical_not(is_self(i)))
        def _():
            send_copy(i).start()

        @pl.when(is_self(i))
        def _():
            pltpu.make_async_copy(
                outgoing.at[i // 8], arrived.at[tile], recv_sem.at[tile]
            ).start()
        return 0

    hear(4)
    lax.fori_loop(0, TILES, send, 0)

    def step_of(a):
        return a + a // 2 - 2 * (a // 3)

    def accumulate(group, total):
        sources = []
        for j in range(4):
            z = lax.rem(along_z + step_of(group // 2), 4)
            x = lax.rem(along_x + step_of(2 * lax.rem(group, 2) + j // 2), 4)
            sources.append((z * 4 + x) * 2 + lax.rem(core + j % 2, 2))
        for t in sources:
            pltpu.make_async_copy(arrived.at[t], arrived.at[t], recv_sem.at[t]).wait()
        for t in sources:
            value = arrived[t]
            for _ in range(2):
                piece = value.astype(jnp.bfloat16)
                value = value - piece.astype(jnp.float32)
                spread = high[t] * jnp.broadcast_to(piece, (128, 512))
                total = total + lax.dot_general(
                    spread, low[t], (((1,), (1,)), ((), ())),
                    preferred_element_type=jnp.float32,
                )
        return total

    sums = lax.fori_loop(0, TILES // 4, accumulate, jnp.zeros((128, 128), jnp.float32))
    flux[...] = sums[: OWNED // 128]

    for group in range(6):
        for copy in edge_copies(group, 1, *edges1) + edge_copies(group, 0, *edges0):
            copy.wait_send()

    @pl.when(lev > 0)
    def _():
        for copy in level_copies(forcing, halo1, 1) + level_copies(field, halo0, 0):
            copy.wait_send()

    for p in range(1, 8):
        reduce_copy(p).wait_send()

    def finish(i, _):
        @pl.when(jnp.logical_not(is_self(i)))
        def _():
            send_copy(i).wait_send()
        return 0

    lax.fori_loop(0, TILES, finish, 0)


def store_kernel(adjoint, flux, adjoint_out, flux_out, sem):
    copies = (
        pltpu.make_async_copy(adjoint, adjoint_out, sem.at[0]),
        pltpu.make_async_copy(flux, flux_out, sem.at[1]),
    )
    for copy in copies:
        copy.start()
    for copy in copies:
        copy.wait()


def shards(
    forcing, courant_x, courant_y, mass_flux, limiter_code, seam_code, level_weight,
    sector_share, flux_cell,
):
    f32, bf16, i32 = jnp.float32, jnp.bfloat16, jnp.int32
    shape = jax.ShapeDtypeStruct
    dma = pltpu.SemaphoreType.DMA
    edge = pltpu.VMEM((LEV, SEC, COLS), f32)
    plane = pltpu.VMEM((SEC, ROWS, COLS), f32)
    levels = (LEV, ROWS, COLS)
    passed = pl.pallas_call(
        adjoint_kernel,
        out_shape=(
            shape(forcing.shape, f32),
            shape((OWNED // 128, 128), f32),
        ),
        in_specs=[HBM] * 9,
        out_specs=[VMEM] * 2,
        scratch_shapes=[pltpu.SMEM((2, TILES), i32), pltpu.SMEM((LEV,), f32)]
        + [pltpu.VMEM(forcing.shape, f32)] * 2
        + [pltpu.VMEM(levels, bf16)] * 3
        + [pltpu.VMEM(levels, i32)]
        + [plane]
        + [pltpu.VMEM((TILES, 480), i32), pltpu.VMEM((TILES, 512), i32)]
        + [plane] * 2
        + [pltpu.VMEM((2, 2, SEC, COLS), f32)] * 2
        + [edge] * 8
        + [
            pltpu.VMEM((ROWS, COLS), f32),
            pltpu.VMEM((8, 5, COLS), f32),
            pltpu.VMEM((7, 5, COLS), f32),
            pltpu.VMEM((4, 1, 512), f32),
            pltpu.VMEM((TILES, 1, 512), f32),
            pltpu.VMEM((TILES, 128, 512), bf16),
            pltpu.VMEM((TILES, 128, 512), bf16),
        ]
        + [dma((5, LEV // 2)), dma((4,)), dma((2, 2)), dma((2, 2)), dma((2, 2, 6)), dma((2, 2, 6))]
        + [dma((7,)), dma((7,)), dma((TILES,)), dma((TILES,))]
        + [pltpu.SemaphoreType.REGULAR((5,))],
        compiler_params=pltpu.CompilerParams(
            collective_id=0, has_side_effects=True, vmem_limit_bytes=LIMIT_FIRST * MIB
        ),
        name="adjoint",
    )(
        *(
            pltpu.with_memory_space_constraint(x, pltpu.HBM)
            for x in (
                seam_code.T, level_weight, forcing, courant_x, courant_y, mass_flux,
                limiter_code, sector_share, flux_cell,
            )
        ),
    )
    adjoint, flux = pl.pallas_call(
        store_kernel,
        out_shape=(shape(forcing.shape, f32), shape((OWNED // 128, 128), f32)),
        in_specs=[VMEM] * 2,
        out_specs=[HBM] * 2,
        scratch_shapes=[dma((2,))],
        compiler_params=pltpu.CompilerParams(vmem_limit_bytes=LIMIT_SECOND * MIB),
        name="store",
    )(*passed)
    return adjoint, flux.reshape(-1)


def solution(mesh):
    placed = (
        P("sec", "lev", "tile", None),
        P("lev", "tile", None),
        P("lev", "tile", None),
        P("lev", "tile", None),
        P("lev", "tile", None),
        P(),
        P("lev"),
        P("sec", "tile", None),
        P("tile", None),
    )
    return jax.shard_map(
        shards,
        mesh=mesh,
        in_specs=placed,
        out_specs=(P("sec", "lev", "tile", None), P("tile")),
        check_vma=False,
    )
```

```python
import functools

import jax
import jax.numpy as jnp
from jax import lax
from jax.experimental import pallas as pl
from jax.experimental.pallas import tpu as pltpu
from jax.sharding import PartitionSpec as P

SEC, LEV, ROWS, COLS = 4, 18, 40, 384
TILES = 32
OWNED = 15360
MESH = pl.DeviceIdType.MESH
HBM = pl.BlockSpec(memory_space=pltpu.HBM)
VMEM = pl.BlockSpec(memory_space=pltpu.VMEM)
SMEM = pl.BlockSpec(memory_space=pltpu.SMEM)
MIB = 1024 * 1024
LIMIT_FIRST = 40
LIMIT_SECOND = 8
CHUNKS = ((0, 16), (16, 16), (32, 8))
REST0_AT = 1


def coefficients(courant, code, bit):
    size = jnp.abs(courant)
    rest = 1.0 - size
    twice = jnp.where((code & (1 << bit)) != 0, size * rest, 0.0)
    spread = 0.5 * twice
    positive = jnp.maximum(courant, 0.0)
    ahead = positive - spread
    back = (size - positive) - spread
    return ahead, back


def second_coefficients(courant, code, bit):
    ahead, back = coefficients(courant, code, bit)
    lane = lax.broadcasted_iota(jnp.int32, ahead.shape, 1)
    ahead = jnp.where(lane == COLS - 1, 0.0, ahead)
    back = jnp.where(lane == 0, 0.0, back)
    return ahead, back, 1.0 - ahead - back


def rims(left, right, flag_left, flag_right):
    both = jnp.concatenate([left, right], axis=0)
    lane = lax.broadcasted_iota(jnp.int32, (2 * SEC, 128), 1)
    parts = [
        jnp.take_along_axis(both[:, i * 128 : (i + 1) * 128], 127 - lane, axis=1)
        for i in (2, 1, 0)
    ]
    row = lax.broadcasted_iota(jnp.int32, both.shape, 0)
    flag = jnp.where(row < SEC, flag_left, flag_right)
    return jnp.where(flag == 1, jnp.concatenate(parts, axis=1), both)


def first_sweep(blocks, edges, sector, coefs):
    sub = lax.broadcasted_iota(jnp.int32, (8, COLS), 0)
    low = jnp.broadcast_to(edges[sector : sector + 1], (8, COLS))
    high = jnp.broadcast_to(edges[SEC + sector : SEC + sector + 1], (8, COLS))
    down = [low] + [pltpu.roll(b, 1, 0) for b in blocks]
    up = [pltpu.roll(b, 7, 0) for b in blocks] + [high]
    out = []
    for i, block in enumerate(blocks):
        ahead, back, centre = coefs[i]
        previous = jnp.where(sub == 0, down[i], down[i + 1])
        following = jnp.where(sub == 7, up[i + 1], up[i])
        out.append(centre * block + ahead * following + back * previous)
    return out


def first_coefficients(courant, code, bit):
    ahead, back = coefficients(courant.astype(jnp.float32), code, bit)
    centre = 1.0 - ahead - back
    return [
        (ahead[i : i + 8], back[i : i + 8], centre[i : i + 8]) for i in range(0, ROWS, 8)
    ]


def adjoint_kernel(
    seam_code,
    level_weight,
    forcing,
    courant_x,
    courant_y,
    mass_flux,
    limiter,
    sector_share,
    flux_cell,
    out,
    flux,
    seam,
    weight,
    field,
    swept,
    cx,
    cy,
    mf,
    code,
    share,
    cells,
    padded,
    halo1,
    halo0,
    rows_out,
    rows_in,
    first1,
    last1,
    left1,
    right1,
    first0,
    last0,
    left0,
    right0,
    total,
    partial,
    others,
    outgoing,
    arrived,
    high,
    low,
    load_sem,
    extra_sem,
    lev_send,
    lev_recv,
    edge_send,
    edge_recv,
    rs_send,
    rs_recv,
    send_sem,
    recv_sem,
    ready,
):
    tile, lev, sec = lax.axis_index("tile"), lax.axis_index("lev"), lax.axis_index("sec")
    after, before = lax.rem(tile + 1, TILES), lax.rem(tile + TILES - 1, TILES)
    lower = lax.rem(lev + 3, 4)
    me = lev * 2 + sec

    def member(q):
        return {"tile": tile, "lev": q // 2, "sec": lax.rem(q, 2)}

    def loads(i):
        pair = pl.ds(2 * i, 2)
        return (
            pltpu.make_async_copy(forcing.at[:, pair], field.at[:, pair], load_sem.at[0, i]),
            pltpu.make_async_copy(mass_flux.at[pair], mf.at[pair], load_sem.at[1, i]),
            pltpu.make_async_copy(courant_y.at[pair], cy.at[pair], load_sem.at[2, i]),
            pltpu.make_async_copy(limiter.at[pair], code.at[pair], load_sem.at[3, i]),
            pltpu.make_async_copy(courant_x.at[pair], cx.at[pair], load_sem.at[4, i]),
        )

    def start_loads(i, _):
        for copy in loads(i)[:4]:
            copy.start()
        return 0

    def start_late_loads(i, _):
        loads(i)[4].start()
        return 0

    share_copy = pltpu.make_async_copy(sector_share, share, extra_sem.at[0])
    cells_copy = pltpu.make_async_copy(flux_cell, cells, extra_sem.at[1])
    seam_copy = pltpu.make_async_copy(seam_code, seam, extra_sem.at[2])
    weight_copy = pltpu.make_async_copy(level_weight, weight, extra_sem.at[3])

    barrier = pltpu.get_barrier_semaphore()
    along_z, along_x, core = tile // 8, lax.rem(tile // 2, 4), lax.rem(tile, 2)

    def tile_at(z, x, c):
        return {"tile": (lax.rem(z, 4) * 4 + lax.rem(x, 4)) * 2 + lax.rem(c, 2)}

    beside_z = [tile_at(along_z + i, along_x, core) for i in (1, 3)]
    beside_x = [tile_at(along_z, along_x + i, core) for i in (1, 3)]
    near = [{"tile": after}, {"tile": before}] + beside_z + beside_x
    near += [member(lax.rem(me + p, 8)) for p in range(1, 8)]
    for device in near:
        pl.semaphore_signal(barrier, inc=1, device_id=device, device_id_type=MESH)

    stages = (beside_z, beside_z, beside_x, beside_x, [tile_at(along_z, along_x, core + 1)])

    def tell(i):
        for device in stages[i]:
            pl.semaphore_signal(ready.at[i], inc=1, device_id=device, device_id_type=MESH)

    def hear(i):
        pl.semaphore_wait(ready.at[i], len(stages[i]))

    lax.fori_loop(0, LEV // 2, start_loads, 0)
    lax.fori_loop(0, LEV // 2, start_late_loads, 0)
    for copy in (share_copy, cells_copy, seam_copy, weight_copy):
        copy.start()

    def level_copies(source, halo, step):
        return (
            pltpu.make_async_remote_copy(
                rows_out.at[step], rows_in.at[step],
                lev_send.at[step, 0], lev_recv.at[step, 0],
                device_id={"lev": lower}, device_id_type=MESH,
            ),
            pltpu.make_async_remote_copy(
                source.at[:, 0], halo, lev_send.at[step, 1], lev_recv.at[step, 1],
                device_id={"lev": lower}, device_id_type=MESH,
            ),
        )

    def edge_copies(group, step, first, last, left, right):
        if isinstance(group, int) and group >= 4:
            part = pl.ds(12 + group, 1)
        else:
            part = pl.ds(4 * group, 4)
        return (
            pltpu.make_async_remote_copy(
                first.at[part], right.at[part],
                edge_send.at[step, 0, group], edge_recv.at[step, 0, group],
                device_id={"tile": before}, device_id_type=MESH,
            ),
            pltpu.make_async_remote_copy(
                last.at[part], left.at[part],
                edge_send.at[step, 1, group], edge_recv.at[step, 1, group],
                device_id={"tile": after}, device_id_type=MESH,
            ),
        )

    def start_levels(source, halo, step):
        for i, row in enumerate((0, ROWS - 1)):
            for s in range(SEC):
                rows_out[step, i, s : s + 1, :] = field[s, 0, row : row + 1, :]

        @pl.when(lev > 0)
        def _():
            for copy in level_copies(source, halo, step):
                copy.start()

    def meet():
        pl.semaphore_wait(barrier, len(near))
        tell(0)

        start_levels(forcing, halo1, 1)

    def vertical_second(k, above, bit, step, first, last, left, right, rims_too=True):
        for start, size in CHUNKS:
            rows = slice(start, start + size)
            mixing = mf[k, rows, :].astype(jnp.float32)
            ahead, back, centre = second_coefficients(
                cy[k, rows, :].astype(jnp.float32), code[k, rows, :], bit
            )
            for s in range(SEC):
                value = field[s, k, rows, :]
                value = value + mixing * (above(s, rows) - value)
                value = (
                    centre * value
                    + ahead * pltpu.roll(value, COLS - 1, 1)
                    + back * pltpu.roll(value, 1, 1)
                )
                swept[s, k, rows, :] = value
                if rims_too and start == 0:
                    first[k, s : s + 1, :] = value[:1]
                if rims_too and start == 32:
                    last[k, s : s + 1, :] = value[7:]

    def send_edges(group, step, edges):
        for copy in edge_copies(group, step, *edges):
            copy.start()

    def take_edges(group, step, edges):
        for copy in edge_copies(group, step, *edges):
            copy.wait_recv()

    edges1 = (first1, last1, left1, right1)
    edges0 = (first0, last0, left0, right0)
    step1 = (3, 1) + edges1
    step0 = (1, 0) + edges0

    def inner_level(k, step_args):
        vertical_second(k, lambda s, rows: field[s, k + 1, rows, :], *step_args)

    loads(0)[0].wait()

    def phase_a(g, _):
        for i in range(2):
            for copy in loads(2 * g + i)[1:4]:
                copy.wait()
            loads(2 * g + i + 1)[0].wait()
        for j in range(4):
            inner_level(4 * g + j, step1)

        @pl.when(g == 0)
        def _():
            meet()

        send_edges(g, 1, edges1)
        return 0

    lax.fori_loop(0, 4, phase_a, 0)
    for copy in loads(8)[1:4]:
        copy.wait()
    inner_level(16, step1)
    send_edges(4, 1, edges1)

    def top_level(source, halo, step, step_args):
        @pl.when(lev < 3)
        def _():
            level_copies(source, halo, step)[1].wait_recv()

        @pl.when(lev == 3)
        def _():
            for s in range(SEC):
                halo[s] = field[s, LEV - 1]

        vertical_second(
            LEV - 1, lambda s, rows: halo[s, rows, :], *step_args, rims_too=False
        )

    def top_rims(source, halo, step, bit, targets):
        @pl.when(lev < 3)
        def _():
            level_copies(source, halo, step)[0].wait_recv()

        for i, (start, at, target) in enumerate(((0, 0, targets[0]), (32, 7, targets[1]))):
            rows = slice(start, start + 8)
            value = jnp.concatenate(
                [field[s, LEV - 1, start + at : start + at + 1, :] for s in range(SEC)], axis=0
            )
            ahead, back, centre = second_coefficients(
                cy[LEV - 1, rows, :].astype(jnp.float32), code[LEV - 1, rows, :], bit
            )
            mixing = mf[LEV - 1, rows, :].astype(jnp.float32)
            ahead, back, centre, mixing = [
                x[at : at + 1] for x in (ahead, back, centre, mixing)
            ]
            above = jnp.where(lev == 3, value, rows_in[step, i])
            value = value + mixing * (above - value)
            target[LEV - 1] = (
                centre * value
                + ahead * pltpu.roll(value, COLS - 1, 1)
                + back * pltpu.roll(value, 1, 1)
            )
        send_edges(5, step, edges1 if step else edges0)

    cells_copy.wait()
    padded[...] = jnp.concatenate(
        [cells[...], jnp.full((TILES, 32), -1, jnp.int32)], axis=1
    )
    slot = lax.broadcasted_iota(jnp.int32, (128, 512), 0)

    def one_hot(t, _):
        cell = padded[pl.ds(t, 1), :]
        high[t] = jnp.where(slot == (cell >> 7), 1.0, 0.0).astype(jnp.bfloat16)
        low[t] = jnp.where(slot == (cell & 127), 1.0, 0.0).astype(jnp.bfloat16)
        return 0

    lax.fori_loop(0, TILES, one_hot, 0)

    seam_copy.wait()
    flag_left, flag_right = seam[0, tile], seam[1, tile]

    def first_dimension(k, edges, bit, target):
        rim = rims(edges[2][k], edges[3][k], flag_left, flag_right)
        coefs = first_coefficients(cx[k], code[k], bit)
        results = []
        for s in range(SEC):
            blocks = [swept[s, k, i : i + 8, :] for i in range(0, ROWS, 8)]
            blocks = first_sweep(blocks, rim, s, coefs)
            for i, block in enumerate(blocks):
                target[s, k, i * 8 : i * 8 + 8, :] = block
            results.append(blocks)
        return results

    hear(0)
    tell(1)

    def first_group(g, least=0):
        if least == 0:
            take_edges(g, 1, edges1)
            for i in range(2):
                loads(2 * g + i)[4].wait()
        for j in range(least, 4):
            first_dimension(4 * g + j, edges1, 2, field)

    def second_group(g):
        for j in range(4):
            inner_level(4 * g + j, step0)
        send_edges(g, 0, edges0)

    top_rims(forcing, halo1, 1, 3, (first1, last1))
    take_edges(0, 1, edges1)
    for i in range(2):
        loads(i)[4].wait()
    first_dimension(0, edges1, 2, field)
    start_levels(field, halo0, 0)
    first_group(0, 1)

    def phase_b(g, _):
        first_group(g + 1)
        second_group(g)

        @pl.when(g == 1)
        def _():
            hear(1)
            tell(2)

        return 0

    lax.fori_loop(0, 3, phase_b, 0)
    take_edges(4, 1, edges1)
    loads(8)[4].wait()
    first_dimension(16, edges1, 2, field)
    second_group(3)
    hear(2)
    tell(3)
    top_level(forcing, halo1, 1, step1)
    take_edges(5, 1, edges1)
    first_dimension(17, edges1, 2, field)
    top_rims(field, halo0, 0, 1, (first0, last0))
    inner_level(16, step0)
    send_edges(4, 0, edges0)

    share_copy.wait()
    weight_copy.wait()
    total[...] = jnp.zeros_like(total)

    def last_level(k):
        results = first_dimension(k, edges0, 0, out)
        for i in range(ROWS // 8):
            rows = slice(i * 8, i * 8 + 8)
            term = share[0, rows, :] * results[0][i]
            for s in range(1, SEC):
                term = term + share[s, rows, :] * results[s][i]
            total[rows, :] += weight[k] * term

    def phase_c(g, _):
        @pl.when(g == REST0_AT)
        def _():
            top_level(field, halo0, 0, step0)

        @pl.when(g == 1)
        def _():
            hear(3)
            tell(4)

        take_edges(g, 0, edges0)
        for j in range(4):
            last_level(4 * g + j)
        return 0

    lax.fori_loop(0, 4, phase_c, 0)
    take_edges(4, 0, edges0)
    last_level(16)
    take_edges(5, 0, edges0)
    last_level(17)

    for q in range(8):
        partial[q] = total[5 * q : 5 * q + 5, :]

    def reduce_copy(p):
        return pltpu.make_async_remote_copy(
            partial.at[lax.rem(me + p, 8)], others.at[p - 1],
            rs_send.at[p - 1], rs_recv.at[p - 1],
            device_id=member(lax.rem(me + p, 8)), device_id_type=MESH,
        )

    for p in range(1, 8):
        reduce_copy(p).start()

    summed = partial[me]
    for p in range(1, 8):
        reduce_copy(p).wait_recv()
        summed = summed + others[p - 1]
    for r in range(4):
        pair = jnp.concatenate([summed[r : r + 1], summed[r + 1 : r + 2]], axis=1)
        if r:
            pair = pltpu.roll(pair, 768 - 96 * r, 1)
        outgoing[r] = pair[:, :512]

    def send_copy(i):
        return pltpu.make_async_remote_copy(
            outgoing.at[i // 8], arrived.at[tile], send_sem.at[i], recv_sem.at[tile],
            device_id={
                "tile": me * 4 + i // 8, "lev": lax.rem(i, 8) // 2, "sec": lax.rem(i, 2),
            },
            device_id_type=MESH,
        )

    def is_self(i):
        return jnp.logical_and(me * 4 + i // 8 == tile, lax.rem(i, 8) == me)

    def send(i, _):
        @pl.when(jnp.logical_not(is_self(i)))
        def _():
            send_copy(i).start()

        @pl.when(is_self(i))
        def _():
            pltpu.make_async_copy(
                outgoing.at[i // 8], arrived.at[tile], recv_sem.at[tile]
            ).start()
        return 0

    hear(4)
    lax.fori_loop(0, TILES, send, 0)

    for group in range(6):
        for copy in edge_copies(group, 1, *edges1) + edge_copies(group, 0, *edges0):
            copy.wait_send()

    @pl.when(lev > 0)
    def _():
        for copy in level_copies(forcing, halo1, 1) + level_copies(field, halo0, 0):
            copy.wait_send()

    for p in range(1, 8):
        reduce_copy(p).wait_send()

    def finish(i, _):
        @pl.when(jnp.logical_not(is_self(i)))
        def _():
            send_copy(i).wait_send()
        return 0

    lax.fori_loop(0, TILES, finish, 0)

    def step_of(a):
        return a + a // 2 - 2 * (a // 3)

    def accumulate(group, total):
        sources = []
        for j in range(4):
            z = lax.rem(along_z + step_of(group // 2), 4)
            x = lax.rem(along_x + step_of(2 * lax.rem(group, 2) + j // 2), 4)
            sources.append((z * 4 + x) * 2 + lax.rem(core + j % 2, 2))
        for t in sources:
            pltpu.make_async_copy(arrived.at[t], arrived.at[t], recv_sem.at[t]).wait()
        for t in sources:
            value = arrived[t]
            for _ in range(2):
                piece = value.astype(jnp.bfloat16)
                value = value - piece.astype(jnp.float32)
                spread = high[t] * jnp.broadcast_to(piece, (128, 512))
                total = total + lax.dot_general(
                    spread, low[t], (((1,), (1,)), ((), ())),
                    preferred_element_type=jnp.float32,
                )
        return total

    sums = lax.fori_loop(0, TILES // 4, accumulate, jnp.zeros((128, 128), jnp.float32))
    flux[...] = sums[: OWNED // 128]


def store_kernel(adjoint, flux, adjoint_out, flux_out, sem):
    copies = (
        pltpu.make_async_copy(adjoint, adjoint_out, sem.at[0]),
        pltpu.make_async_copy(flux, flux_out, sem.at[1]),
    )
    for copy in copies:
        copy.start()
    for copy in copies:
        copy.wait()


def shards(
    forcing, courant_x, courant_y, mass_flux, limiter_code, seam_code, level_weight,
    sector_share, flux_cell,
):
    f32, bf16, i32 = jnp.float32, jnp.bfloat16, jnp.int32
    shape = jax.ShapeDtypeStruct
    dma = pltpu.SemaphoreType.DMA
    edge = pltpu.VMEM((LEV, SEC, COLS), f32)
    plane = pltpu.VMEM((SEC, ROWS, COLS), f32)
    levels = (LEV, ROWS, COLS)
    passed = pl.pallas_call(
        adjoint_kernel,
        out_shape=(
            shape(forcing.shape, f32),
            shape((OWNED // 128, 128), f32),
        ),
        in_specs=[HBM] * 9,
        out_specs=[VMEM] * 2,
        scratch_shapes=[pltpu.SMEM((2, TILES), i32), pltpu.SMEM((LEV,), f32)]
        + [pltpu.VMEM(forcing.shape, f32)] * 2
        + [pltpu.VMEM(levels, bf16)] * 3
        + [pltpu.VMEM(levels, i32)]
        + [plane]
        + [pltpu.VMEM((TILES, 480), i32), pltpu.VMEM((TILES, 512), i32)]
        + [plane] * 2
        + [pltpu.VMEM((2, 2, SEC, COLS), f32)] * 2
        + [edge] * 8
        + [
            pltpu.VMEM((ROWS, COLS), f32),
            pltpu.VMEM((8, 5, COLS), f32),
            pltpu.VMEM((7, 5, COLS), f32),
            pltpu.VMEM((4, 1, 512), f32),
            pltpu.VMEM((TILES, 1, 512), f32),
            pltpu.VMEM((TILES, 128, 512), bf16),
            pltpu.VMEM((TILES, 128, 512), bf16),
        ]
        + [dma((5, LEV // 2)), dma((4,)), dma((2, 2)), dma((2, 2)), dma((2, 2, 6)), dma((2, 2, 6))]
        + [dma((7,)), dma((7,)), dma((TILES,)), dma((TILES,))]
        + [pltpu.SemaphoreType.REGULAR((5,))],
        compiler_params=pltpu.CompilerParams(
            collective_id=0, has_side_effects=True, vmem_limit_bytes=LIMIT_FIRST * MIB
        ),
        name="adjoint",
    )(
        *(
            pltpu.with_memory_space_constraint(x, pltpu.HBM)
            for x in (
                seam_code.T, level_weight, forcing, courant_x, courant_y, mass_flux,
                limiter_code, sector_share, flux_cell,
            )
        ),
    )
    adjoint, flux = pl.pallas_call(
        store_kernel,
        out_shape=(shape(forcing.shape, f32), shape((OWNED // 128, 128), f32)),
        in_specs=[VMEM] * 2,
        out_specs=[HBM] * 2,
        scratch_shapes=[dma((2,))],
        compiler_params=pltpu.CompilerParams(vmem_limit_bytes=LIMIT_SECOND * MIB),
        name="store",
    )(*passed)
    return adjoint, flux.reshape(-1)


def solution(mesh):
    placed = (
        P("sec", "lev", "tile", None),
        P("lev", "tile", None),
        P("lev", "tile", None),
        P("lev", "tile", None),
        P("lev", "tile", None),
        P(),
        P("lev"),
        P("sec", "tile", None),
        P("tile", None),
    )
    return jax.shard_map(
        shards,
        mesh=mesh,
        in_specs=placed,
        out_specs=(P("sec", "lev", "tile", None), P("tile")),
        check_vma=False,
    )
```

```python
import functools

import jax
import jax.numpy as jnp
from jax import lax
from jax.experimental import pallas as pl
from jax.experimental.pallas import tpu as pltpu
from jax.sharding import PartitionSpec as P

SEC, LEV, ROWS, COLS = 4, 18, 40, 384
TILES = 32
OWNED = 15360
MESH = pl.DeviceIdType.MESH
HBM = pl.BlockSpec(memory_space=pltpu.HBM)
VMEM = pl.BlockSpec(memory_space=pltpu.VMEM)
SMEM = pl.BlockSpec(memory_space=pltpu.SMEM)
MIB = 1024 * 1024
LIMIT_FIRST = 40
LIMIT_SECOND = 8
CHUNKS = ((0, 16), (16, 16), (32, 8))
REST0_AT = 1


def coefficients(courant, code, bit):
    size = jnp.abs(courant)
    rest = 1.0 - size
    twice = jnp.where((code & (1 << bit)) != 0, size * rest, 0.0)
    spread = 0.5 * twice
    positive = jnp.maximum(courant, 0.0)
    ahead = positive - spread
    back = (size - positive) - spread
    return ahead, back


def second_coefficients(courant, code, bit):
    ahead, back = coefficients(courant, code, bit)
    lane = lax.broadcasted_iota(jnp.int32, ahead.shape, 1)
    ahead = jnp.where(lane == COLS - 1, 0.0, ahead)
    back = jnp.where(lane == 0, 0.0, back)
    return ahead, back, 1.0 - ahead - back


def rims(left, right, flag_left, flag_right):
    both = jnp.concatenate([left, right], axis=0)
    lane = lax.broadcasted_iota(jnp.int32, (2 * SEC, 128), 1)
    parts = [
        jnp.take_along_axis(both[:, i * 128 : (i + 1) * 128], 127 - lane, axis=1)
        for i in (2, 1, 0)
    ]
    row = lax.broadcasted_iota(jnp.int32, both.shape, 0)
    flag = jnp.where(row < SEC, flag_left, flag_right)
    return jnp.where(flag == 1, jnp.concatenate(parts, axis=1), both)


def first_sweep(blocks, edges, sector, coefs):
    sub = lax.broadcasted_iota(jnp.int32, (8, COLS), 0)
    low = jnp.broadcast_to(edges[sector : sector + 1], (8, COLS))
    high = jnp.broadcast_to(edges[SEC + sector : SEC + sector + 1], (8, COLS))
    down = [low] + [pltpu.roll(b, 1, 0) for b in blocks]
    up = [pltpu.roll(b, 7, 0) for b in blocks] + [high]
    out = []
    for i, block in enumerate(blocks):
        ahead, back, centre = coefs[i]
        previous = jnp.where(sub == 0, down[i], down[i + 1])
        following = jnp.where(sub == 7, up[i + 1], up[i])
        out.append(centre * block + ahead * following + back * previous)
    return out


def first_coefficients(courant, code, bit):
    ahead, back = coefficients(courant.astype(jnp.float32), code, bit)
    centre = 1.0 - ahead - back
    return [
        (ahead[i : i + 8], back[i : i + 8], centre[i : i + 8]) for i in range(0, ROWS, 8)
    ]


def adjoint_kernel(
    seam_code,
    level_weight,
    forcing,
    courant_x,
    courant_y,
    mass_flux,
    limiter,
    sector_share,
    flux_cell,
    out,
    flux,
    seam,
    weight,
    field,
    swept,
    cx,
    cy,
    mf,
    code,
    share,
    cells,
    padded,
    halo1,
    halo0,
    rows_out,
    rows_in,
    first1,
    last1,
    left1,
    right1,
    first0,
    last0,
    left0,
    right0,
    total,
    partial,
    others,
    outgoing,
    arrived,
    high,
    low,
    load_sem,
    extra_sem,
    lev_send,
    lev_recv,
    edge_send,
    edge_recv,
    rs_send,
    rs_recv,
    send_sem,
    recv_sem,
    ready,
):
    tile, lev, sec = lax.axis_index("tile"), lax.axis_index("lev"), lax.axis_index("sec")
    after, before = lax.rem(tile + 1, TILES), lax.rem(tile + TILES - 1, TILES)
    lower = lax.rem(lev + 3, 4)
    me = lev * 2 + sec

    def member(q):
        return {"tile": tile, "lev": q // 2, "sec": lax.rem(q, 2)}

    def loads(i):
        pair = pl.ds(2 * i, 2)
        return (
            pltpu.make_async_copy(forcing.at[:, pair], field.at[:, pair], load_sem.at[0, i]),
            pltpu.make_async_copy(mass_flux.at[pair], mf.at[pair], load_sem.at[1, i]),
            pltpu.make_async_copy(courant_y.at[pair], cy.at[pair], load_sem.at[2, i]),
            pltpu.make_async_copy(limiter.at[pair], code.at[pair], load_sem.at[3, i]),
            pltpu.make_async_copy(courant_x.at[pair], cx.at[pair], load_sem.at[4, i]),
        )

    def start_loads(i, _):
        for copy in loads(i)[:4]:
            copy.start()
        return 0

    def start_late_loads(i, _):
        loads(i)[4].start()
        return 0

    share_copy = pltpu.make_async_copy(sector_share, share, extra_sem.at[0])
    cells_copy = pltpu.make_async_copy(flux_cell, cells, extra_sem.at[1])
    seam_copy = pltpu.make_async_copy(seam_code, seam, extra_sem.at[2])
    weight_copy = pltpu.make_async_copy(level_weight, weight, extra_sem.at[3])

    barrier = pltpu.get_barrier_semaphore()
    along_z, along_x, core = tile // 8, lax.rem(tile // 2, 4), lax.rem(tile, 2)

    def tile_at(z, x, c):
        return {"tile": (lax.rem(z, 4) * 4 + lax.rem(x, 4)) * 2 + lax.rem(c, 2)}

    beside_z = [tile_at(along_z + i, along_x, core) for i in (1, 3)]
    beside_x = [tile_at(along_z, along_x + i, core) for i in (1, 3)]
    near = [member(lax.rem(me + p, 8)) for p in range(1, 8)]
    near += [{"tile": after}, {"tile": before}] + beside_z + beside_x
    for device in near:
        pl.semaphore_signal(barrier, inc=1, device_id=device, device_id_type=MESH)

    stages = (beside_z, beside_z, beside_x, beside_x, [tile_at(along_z, along_x, core + 1)])

    def tell(i):
        for device in stages[i]:
            pl.semaphore_signal(ready.at[i], inc=1, device_id=device, device_id_type=MESH)

    def hear(i):
        pl.semaphore_wait(ready.at[i], len(stages[i]))

    lax.fori_loop(0, LEV // 2, start_loads, 0)
    lax.fori_loop(0, LEV // 2, start_late_loads, 0)
    for copy in (share_copy, cells_copy, seam_copy, weight_copy):
        copy.start()

    def level_copies(source, halo, step):
        return (
            pltpu.make_async_remote_copy(
                rows_out.at[step], rows_in.at[step],
                lev_send.at[step, 0], lev_recv.at[step, 0],
                device_id={"lev": lower}, device_id_type=MESH,
            ),
            pltpu.make_async_remote_copy(
                source.at[:, 0], halo, lev_send.at[step, 1], lev_recv.at[step, 1],
                device_id={"lev": lower}, device_id_type=MESH,
            ),
        )

    def edge_copies(group, step, first, last, left, right):
        if isinstance(group, int) and group >= 4:
            part = pl.ds(12 + group, 1)
        else:
            part = pl.ds(4 * group, 4)
        return (
            pltpu.make_async_remote_copy(
                first.at[part], right.at[part],
                edge_send.at[step, 0, group], edge_recv.at[step, 0, group],
                device_id={"tile": before}, device_id_type=MESH,
            ),
            pltpu.make_async_remote_copy(
                last.at[part], left.at[part],
                edge_send.at[step, 1, group], edge_recv.at[step, 1, group],
                device_id={"tile": after}, device_id_type=MESH,
            ),
        )

    def start_levels(source, halo, step):
        for i, row in enumerate((0, ROWS - 1)):
            for s in range(SEC):
                rows_out[step, i, s : s + 1, :] = field[s, 0, row : row + 1, :]

        @pl.when(lev > 0)
        def _():
            for copy in level_copies(source, halo, step):
                copy.start()

    def meet():
        pl.semaphore_wait(barrier, len(near))
        tell(0)

        start_levels(forcing, halo1, 1)

    def vertical_second(k, above, bit, step, first, last, left, right, rims_too=True):
        for start, size in CHUNKS:
            rows = slice(start, start + size)
            mixing = mf[k, rows, :].astype(jnp.float32)
            ahead, back, centre = second_coefficients(
                cy[k, rows, :].astype(jnp.float32), code[k, rows, :], bit
            )
            for s in range(SEC):
                value = field[s, k, rows, :]
                value = value + mixing * (above(s, rows) - value)
                value = (
                    centre * value
                    + ahead * pltpu.roll(value, COLS - 1, 1)
                    + back * pltpu.roll(value, 1, 1)
                )
                swept[s, k, rows, :] = value
                if rims_too and start == 0:
                    first[k, s : s + 1, :] = value[:1]
                if rims_too and start == 32:
                    last[k, s : s + 1, :] = value[7:]

    def send_edges(group, step, edges):
        for copy in edge_copies(group, step, *edges):
            copy.start()

    def take_edges(group, step, edges):
        for copy in edge_copies(group, step, *edges):
            copy.wait_recv()

    edges1 = (first1, last1, left1, right1)
    edges0 = (first0, last0, left0, right0)
    step1 = (3, 1) + edges1
    step0 = (1, 0) + edges0

    def inner_level(k, step_args):
        vertical_second(k, lambda s, rows: field[s, k + 1, rows, :], *step_args)

    loads(0)[0].wait()

    def phase_a(g, _):
        for i in range(2):
            for copy in loads(2 * g + i)[1:4]:
                copy.wait()
            loads(2 * g + i + 1)[0].wait()
        for j in range(4):
            inner_level(4 * g + j, step1)

        @pl.when(g == 0)
        def _():
            meet()

        send_edges(g, 1, edges1)
        return 0

    lax.fori_loop(0, 4, phase_a, 0)
    for copy in loads(8)[1:4]:
        copy.wait()
    inner_level(16, step1)
    send_edges(4, 1, edges1)

    def top_level(source, halo, step, step_args):
        @pl.when(lev < 3)
        def _():
            level_copies(source, halo, step)[1].wait_recv()

        @pl.when(lev == 3)
        def _():
            for s in range(SEC):
                halo[s] = field[s, LEV - 1]

        vertical_second(
            LEV - 1, lambda s, rows: halo[s, rows, :], *step_args, rims_too=False
        )

    def top_rims(source, halo, step, bit, targets):
        @pl.when(lev < 3)
        def _():
            level_copies(source, halo, step)[0].wait_recv()

        for i, (start, at, target) in enumerate(((0, 0, targets[0]), (32, 7, targets[1]))):
            rows = slice(start, start + 8)
            value = jnp.concatenate(
                [field[s, LEV - 1, start + at : start + at + 1, :] for s in range(SEC)], axis=0
            )
            ahead, back, centre = second_coefficients(
                cy[LEV - 1, rows, :].astype(jnp.float32), code[LEV - 1, rows, :], bit
            )
            mixing = mf[LEV - 1, rows, :].astype(jnp.float32)
            ahead, back, centre, mixing = [
                x[at : at + 1] for x in (ahead, back, centre, mixing)
            ]
            above = jnp.where(lev == 3, value, rows_in[step, i])
            value = value + mixing * (above - value)
            target[LEV - 1] = (
                centre * value
                + ahead * pltpu.roll(value, COLS - 1, 1)
                + back * pltpu.roll(value, 1, 1)
            )
        send_edges(5, step, edges1 if step else edges0)

    cells_copy.wait()
    padded[...] = jnp.concatenate(
        [cells[...], jnp.full((TILES, 32), -1, jnp.int32)], axis=1
    )
    slot = lax.broadcasted_iota(jnp.int32, (128, 512), 0)

    def one_hot(t, _):
        cell = padded[pl.ds(t, 1), :]
        high[t] = jnp.where(slot == (cell >> 7), 1.0, 0.0).astype(jnp.bfloat16)
        low[t] = jnp.where(slot == (cell & 127), 1.0, 0.0).astype(jnp.bfloat16)
        return 0

    lax.fori_loop(0, TILES, one_hot, 0)

    seam_copy.wait()
    flag_left, flag_right = seam[0, tile], seam[1, tile]

    def first_dimension(k, edges, bit, target):
        rim = rims(edges[2][k], edges[3][k], flag_left, flag_right)
        coefs = first_coefficients(cx[k], code[k], bit)
        results = []
        for s in range(SEC):
            blocks = [swept[s, k, i : i + 8, :] for i in range(0, ROWS, 8)]
            blocks = first_sweep(blocks, rim, s, coefs)
            for i, block in enumerate(blocks):
                target[s, k, i * 8 : i * 8 + 8, :] = block
            results.append(blocks)
        return results

    hear(0)
    tell(1)

    def first_group(g, least=0):
        if least == 0:
            take_edges(g, 1, edges1)
            for i in range(2):
                loads(2 * g + i)[4].wait()
        for j in range(least, 4):
            first_dimension(4 * g + j, edges1, 2, field)

    def second_group(g):
        for j in range(4):
            inner_level(4 * g + j, step0)
        send_edges(g, 0, edges0)

    top_rims(forcing, halo1, 1, 3, (first1, last1))
    take_edges(0, 1, edges1)
    for i in range(2):
        loads(i)[4].wait()
    first_dimension(0, edges1, 2, field)
    start_levels(field, halo0, 0)
    first_group(0, 1)

    def phase_b(g, _):
        first_group(g + 1)
        second_group(g)

        @pl.when(g == 1)
        def _():
            hear(1)
            tell(2)

        return 0

    lax.fori_loop(0, 3, phase_b, 0)
    take_edges(4, 1, edges1)
    loads(8)[4].wait()
    first_dimension(16, edges1, 2, field)
    second_group(3)
    hear(2)
    tell(3)
    top_level(forcing, halo1, 1, step1)
    take_edges(5, 1, edges1)
    first_dimension(17, edges1, 2, field)
    top_rims(field, halo0, 0, 1, (first0, last0))
    inner_level(16, step0)
    send_edges(4, 0, edges0)

    share_copy.wait()
    weight_copy.wait()
    total[...] = jnp.zeros_like(total)

    def last_level(k):
        results = first_dimension(k, edges0, 0, out)
        for i in range(ROWS // 8):
            rows = slice(i * 8, i * 8 + 8)
            term = share[0, rows, :] * results[0][i]
            for s in range(1, SEC):
                term = term + share[s, rows, :] * results[s][i]
            total[rows, :] += weight[k] * term

    def phase_c(g, _):
        @pl.when(g == REST0_AT)
        def _():
            top_level(field, halo0, 0, step0)

        @pl.when(g == 1)
        def _():
            hear(3)
            tell(4)

        take_edges(g, 0, edges0)
        for j in range(4):
            last_level(4 * g + j)
        return 0

    lax.fori_loop(0, 4, phase_c, 0)
    take_edges(4, 0, edges0)
    last_level(16)
    take_edges(5, 0, edges0)
    last_level(17)

    for q in range(8):
        partial[q] = total[5 * q : 5 * q + 5, :]

    def reduce_copy(p):
        return pltpu.make_async_remote_copy(
            partial.at[lax.rem(me + p, 8)], others.at[p - 1],
            rs_send.at[p - 1], rs_recv.at[p - 1],
            device_id=member(lax.rem(me + p, 8)), device_id_type=MESH,
        )

    for p in range(1, 8):
        reduce_copy(p).start()

    summed = partial[me]
    for p in range(1, 8):
        reduce_copy(p).wait_recv()
        summed = summed + others[p - 1]
    for r in range(4):
        pair = jnp.concatenate([summed[r : r + 1], summed[r + 1 : r + 2]], axis=1)
        if r:
            pair = pltpu.roll(pair, 768 - 96 * r, 1)
        outgoing[r] = pair[:, :512]

    def goal(i):
        return me * 4 + lax.rem(i, 4), lax.rem(lev + 2 + i // 8, 4), lax.rem(i // 4, 2)

    def send_copy(i):
        to_tile, to_lev, to_sec = goal(i)
        return pltpu.make_async_remote_copy(
            outgoing.at[lax.rem(i, 4)], arrived.at[tile], send_sem.at[i], recv_sem.at[tile],
            device_id={"tile": to_tile, "lev": to_lev, "sec": to_sec},
            device_id_type=MESH,
        )

    def is_self(i):
        to_tile, to_lev, to_sec = goal(i)
        return jnp.logical_and(
            to_tile == tile, jnp.logical_and(to_lev == lev, to_sec == sec)
        )

    def send(i, _):
        @pl.when(jnp.logical_not(is_self(i)))
        def _():
            send_copy(i).start()

        @pl.when(is_self(i))
        def _():
            pltpu.make_async_copy(
                outgoing.at[lax.rem(i, 4)], arrived.at[tile], recv_sem.at[tile]
            ).start()
        return 0

    hear(4)
    lax.fori_loop(0, TILES, send, 0)

    for group in range(6):
        for copy in edge_copies(group, 1, *edges1) + edge_copies(group, 0, *edges0):
            copy.wait_send()

    @pl.when(lev > 0)
    def _():
        for copy in level_copies(forcing, halo1, 1) + level_copies(field, halo0, 0):
            copy.wait_send()

    for p in range(1, 8):
        reduce_copy(p).wait_send()

    def finish(i, _):
        @pl.when(jnp.logical_not(is_self(i)))
        def _():
            send_copy(i).wait_send()
        return 0

    lax.fori_loop(0, TILES, finish, 0)

    def step_of(a):
        return a + a // 2 - 2 * (a // 3)

    def accumulate(group, total):
        sources = []
        for j in range(4):
            z = lax.rem(along_z + step_of(group // 2), 4)
            x = lax.rem(along_x + step_of(2 * lax.rem(group, 2) + j // 2), 4)
            sources.append((z * 4 + x) * 2 + lax.rem(core + j % 2, 2))
        for t in sources:
            pltpu.make_async_copy(arrived.at[t], arrived.at[t], recv_sem.at[t]).wait()
        for t in sources:
            value = arrived[t]
            for _ in range(2):
                piece = value.astype(jnp.bfloat16)
                value = value - piece.astype(jnp.float32)
                spread = high[t] * jnp.broadcast_to(piece, (128, 512))
                total = total + lax.dot_general(
                    spread, low[t], (((1,), (1,)), ((), ())),
                    preferred_element_type=jnp.float32,
                )
        return total

    sums = lax.fori_loop(0, TILES // 4, accumulate, jnp.zeros((128, 128), jnp.float32))
    flux[...] = sums[: OWNED // 128]


def store_kernel(adjoint, flux, adjoint_out, flux_out, sem):
    copies = (
        pltpu.make_async_copy(adjoint, adjoint_out, sem.at[0]),
        pltpu.make_async_copy(flux, flux_out, sem.at[1]),
    )
    for copy in copies:
        copy.start()
    for copy in copies:
        copy.wait()


def shards(
    forcing, courant_x, courant_y, mass_flux, limiter_code, seam_code, level_weight,
    sector_share, flux_cell,
):
    f32, bf16, i32 = jnp.float32, jnp.bfloat16, jnp.int32
    shape = jax.ShapeDtypeStruct
    dma = pltpu.SemaphoreType.DMA
    edge = pltpu.VMEM((LEV, SEC, COLS), f32)
    plane = pltpu.VMEM((SEC, ROWS, COLS), f32)
    levels = (LEV, ROWS, COLS)
    passed = pl.pallas_call(
        adjoint_kernel,
        out_shape=(
            shape(forcing.shape, f32),
            shape((OWNED // 128, 128), f32),
        ),
        in_specs=[HBM] * 9,
        out_specs=[VMEM] * 2,
        scratch_shapes=[pltpu.SMEM((2, TILES), i32), pltpu.SMEM((LEV,), f32)]
        + [pltpu.VMEM(forcing.shape, f32)] * 2
        + [pltpu.VMEM(levels, bf16)] * 3
        + [pltpu.VMEM(levels, i32)]
        + [plane]
        + [pltpu.VMEM((TILES, 480), i32), pltpu.VMEM((TILES, 512), i32)]
        + [plane] * 2
        + [pltpu.VMEM((2, 2, SEC, COLS), f32)] * 2
        + [edge] * 8
        + [
            pltpu.VMEM((ROWS, COLS), f32),
            pltpu.VMEM((8, 5, COLS), f32),
            pltpu.VMEM((7, 5, COLS), f32),
            pltpu.VMEM((4, 1, 512), f32),
            pltpu.VMEM((TILES, 1, 512), f32),
            pltpu.VMEM((TILES, 128, 512), bf16),
            pltpu.VMEM((TILES, 128, 512), bf16),
        ]
        + [dma((5, LEV // 2)), dma((4,)), dma((2, 2)), dma((2, 2)), dma((2, 2, 6)), dma((2, 2, 6))]
        + [dma((7,)), dma((7,)), dma((TILES,)), dma((TILES,))]
        + [pltpu.SemaphoreType.REGULAR((5,))],
        compiler_params=pltpu.CompilerParams(
            collective_id=0, has_side_effects=True, vmem_limit_bytes=LIMIT_FIRST * MIB
        ),
        name="adjoint",
    )(
        *(
            pltpu.with_memory_space_constraint(x, pltpu.HBM)
            for x in (
                seam_code.T, level_weight, forcing, courant_x, courant_y, mass_flux,
                limiter_code, sector_share, flux_cell,
            )
        ),
    )
    adjoint, flux = pl.pallas_call(
        store_kernel,
        out_shape=(shape(forcing.shape, f32), shape((OWNED // 128, 128), f32)),
        in_specs=[VMEM] * 2,
        out_specs=[HBM] * 2,
        scratch_shapes=[dma((2,))],
        compiler_params=pltpu.CompilerParams(vmem_limit_bytes=LIMIT_SECOND * MIB),
        name="store",
    )(*passed)
    return adjoint, flux.reshape(-1)


def solution(mesh):
    placed = (
        P("sec", "lev", "tile", None),
        P("lev", "tile", None),
        P("lev", "tile", None),
        P("lev", "tile", None),
        P("lev", "tile", None),
        P(),
        P("lev"),
        P("sec", "tile", None),
        P("tile", None),
    )
    return jax.shard_map(
        shards,
        mesh=mesh,
        in_specs=placed,
        out_specs=(P("sec", "lev", "tile", None), P("tile")),
        check_vma=False,
    )
```
